32 devices in a mesh: rcv: 4 (over z), src: 8 (over y, x, core).
Axes of the slice: x: 2, y: 2, z: 4, core: 2. Of those that a mesh axis runs over, the one named last changes fastest.
Arguments:
- reflection: bfloat16 [2, 16384, 16384], P(None, 'rcv', 'src'), may hold values from -6 to 6
- green: bfloat16 [2, 16384, 512], P(None, 'rcv', 'src'), may hold values from -0.046875 to 0.046875
- tile_mask: int32 [64, 64], replicated, may hold values from 0 to 1, as said below
- reference_index: int32 [512], P(('rcv', 'src')), may hold values from 0 to 511
Outputs:
- aligned: float32 [512, 2, 512], P(('rcv', 'src'))
The draws below stay inside these ranges and needn't reach their ends.
Inputs may be any that keep to these rules, and one draw needn't show every extreme that they name: `tile_mask`: entries below the diagonal are 0.
All inputs are finite; a program needn't handle non-finite values.
Results may differ from the reference program's by a relative error of at most 0.02.
Values may be sent and summed in bfloat16 or wider, within the bound.
A program may use at most 256 MiB of HBM per device.

```python
import jax
import jax.numpy as jnp
from jax import lax

S = 16384
P_SIZE = 512
TILE = 256
TILES = 64
N_RCV = 4


def draw_tile_mask(key, part):
    levels = jax.random.randint(jax.random.fold_in(key, 17), (TILES, TILES), 0, 4)
    upper = jnp.arange(TILES)[:, None] <= jnp.arange(TILES)[None, :]
    return ((levels > 0) & upper).astype(jnp.int32)


def place_ends(result, stream_key, low, top_value):
    longest = result.shape.index(max(result.shape))
    spots = []
    for shift in (0, 1):
        where = [jax.random.randint(jax.random.fold_in(stream_key, axis), (), 0, length) for axis, length in enumerate(result.shape)]
        where[longest] = (where[longest] + shift) % result.shape[longest]
        spots.append(tuple(where))
    return result.at[spots[0]].set(low).at[spots[1]].set(top_value)


def block_levels(stream_key, extent, split, least, top_value):
    gain, own = 1.0, jax.random.fold_in(stream_key, 6)
    for dim, blocks in split:
        draws = jnp.exp(jax.random.uniform(jax.random.fold_in(own, dim), (blocks,), jnp.float32, least / len(split), top_value / len(split)))
        gain = gain * jnp.repeat(draws, extent[dim] // blocks).reshape([-1 if axis == dim else 1 for axis in range(len(extent))])
    return gain


def bell_draw(stream_key, shape, spread, reach, pieces=(), held_as=jnp.bfloat16):
    drawn = jax.random.normal(stream_key, shape, jnp.float32) * spread
    if len(pieces) > 0:
        drawn = block_levels(stream_key, shape, pieces, -0.22, 0.18) * drawn
    return jnp.clip(drawn, min=-reach, max=reach).astype(held_as)


def setup_inputs(seed: int = 0) -> dict:
    key_of = jax.random.split(jax.random.key(seed), 5)
    return {
        "reflection": bell_draw(key_of[0], (2, S, S), 1.0, 6.0, ((1, 4), (2, 8))),
        "green": bell_draw(key_of[1], (2, S, P_SIZE), S ** -0.5, 0.046875, ((1, 4), (2, 8))),
        "tile_mask": draw_tile_mask(jax.random.fold_in(key_of[4], 71), 0),
        "reference_index": place_ends(jax.random.randint(key_of[3], (P_SIZE,), 0, P_SIZE), jax.random.fold_in(key_of[3], 1), 0, P_SIZE - 1).astype(jnp.int32),
    }


exact_mode = lax.Precision.HIGHEST


def across(first, second):
    return lax.dot_general(first, second, (((0,), (0,)), ((), ())), preferred_element_type=jnp.float32)


def matmul(first, second):
    return jnp.dot(first, second, precision=exact_mode, preferred_element_type=jnp.float32)


def settle(value):
    return lax.optimization_barrier(value.astype(jnp.bfloat16)).astype(jnp.float32)


def reference(reflection, green, tile_mask, reference_index):
    block_rows = S // N_RCV
    tile_rows = block_rows // TILE
    col_tiles = jnp.arange(S // TILE)
    zero_value = jnp.zeros((), jnp.bfloat16)
    front_real = jnp.zeros((P_SIZE, S), jnp.float32)
    front_imag = jnp.zeros((P_SIZE, S), jnp.float32)
    back_real = jnp.zeros((P_SIZE, S), jnp.float32)
    back_imag = jnp.zeros((P_SIZE, S), jnp.float32)
    for block_index in range(N_RCV):
        row_start = block_index * block_rows
        measured = reflection[:, row_start:row_start + block_rows, :]
        tile_block = tile_mask[block_index * tile_rows:(block_index + 1) * tile_rows, :]
        row_tiles = block_index * tile_rows + jnp.arange(tile_rows)
        kept_tiles = tile_block == 1
        off_diag = kept_tiles & (row_tiles[:, None] != col_tiles[None, :])
        shaped = measured.reshape(2, tile_rows, TILE, S // TILE, TILE)
        acquired = jnp.where(kept_tiles[None, :, None, :, None], shaped, zero_value).reshape(2, block_rows, S)
        mirror_part = jnp.where(off_diag[None, :, None, :, None], shaped, zero_value).reshape(2, block_rows, S)
        green_real = green[0, row_start:row_start + block_rows, :]
        green_imag = green[1, row_start:row_start + block_rows, :]
        front_real = front_real + settle(across(green_real, acquired[0]) + across(green_imag, acquired[1]))
        front_imag = front_imag + settle(across(green_real, acquired[1]) - across(green_imag, acquired[0]))
        back_real = back_real + settle(across(green_real, mirror_part[0]) - across(green_imag, mirror_part[1]))
        back_imag = back_imag + settle(across(green_real, mirror_part[1]) + across(green_imag, mirror_part[0]))
    full_real = green[0].astype(jnp.float32)
    full_imag = green[1].astype(jnp.float32)
    focal_real = matmul(front_real, full_real) - matmul(front_imag, full_imag)
    focal_real = focal_real + (matmul(back_real, full_real) + matmul(back_imag, full_imag)).T
    focal_imag = matmul(front_real, full_imag) + matmul(front_imag, full_real)
    focal_imag = focal_imag + (matmul(back_imag, full_real) - matmul(back_real, full_imag)).T
    chosen = jnp.arange(P_SIZE).astype(jnp.int32)[None, :] == reference_index.astype(jnp.int32)[:, None]
    anchor_real = jnp.sum(jnp.where(chosen, focal_real, 0.0), axis=1)[:, None]
    anchor_imag = jnp.sum(jnp.where(chosen, focal_imag, 0.0), axis=1)[:, None]
    out_real = focal_real * anchor_real + focal_imag * anchor_imag
    out_imag = focal_imag * anchor_real - focal_real * anchor_imag
    return jnp.stack([out_real, out_imag], axis=1)
```

```python
import functools

import jax
import jax.numpy as jnp
from jax import lax
from jax.experimental import pallas as pl
from jax.experimental.pallas import tpu as pltpu
from jax.sharding import PartitionSpec as P

MESH = pl.DeviceIdType.MESH
TILE = 256
f32 = jnp.float32
bf16 = jnp.bfloat16


def dot_nn(a, b):
    return lax.dot_general(a, b, (((1,), (0,)), ((), ())), preferred_element_type=f32)


def dot_nt(a, b):
    return lax.dot_general(a, b, (((1,), (1,)), ((), ())), preferred_element_type=f32)


class Plan:
    def __init__(self, n):
        self.n = n
        self.row = {}
        self.col = {}
        self.relay = {}
        self.down = {}
        self.passes = [{}, {}, {}]
        self.order = {}
        chips = [(z, c) for z in range(n) for c in range(n)]
        for z, c in chips:
            self.row[z, c] = []
            self.col[z, c] = []
            self.order[z, c] = list(range(n))
        if n == 4:
            self.plan_4()
        else:
            for z, c in chips:
                self.row[z, c] = [t for t in sorted(range(z, n), key=lambda t: t ^ c) if t != c]
                self.col[z, c] = [(t, z, c) for t in range(z)]
        waited = {chip: {op[0] for stage in self.passes for op in stage.get(chip, []) if op[4]} for chip in chips}
        self.waits = {chip: [int(q not in waited[chip]) for q in self.order[chip]] for chip in chips}

    def plan_4(self):
        via = {0: 2, 1: 3, 2: 3, 3: 1}
        for z in range(4):
            for q in range(4):
                for j in (1, 2, 3):
                    t = q ^ j
                    if t < z:
                        continue
                    hop = via[q]
                    if j < 3 or hop < z or (z == 2 and q == 0) or z == 3:
                        self.row[z, q].append(t)
                    else:
                        self.relay.setdefault(((z, hop), hop ^ q), []).append(t)
        col = self.col
        for b in (1, 2, 3):
            col[b, b].append((0, b, b))
        col[1, 0].append((0, 1, 0))
        col[2, 0].append((1, 0, 2))
        col[3, 0].append((1, 0, 3))
        col[2, 1].append((1, 2, 1))
        col[3, 1].append((1, 3, 1))
        col[3, 0].append((2, 3, 0))
        col[3, 2].append((2, 3, 2))
        col[3, 3].append((3, 2, 3))
        for b in (1, 2, 3):
            for q in (1, 2, 3):
                if q != b:
                    self.down[(b, b), b ^ q] = [0]
        a, b, _ = self.passes
        a[1, 0] = [(2, 0, 2, 0, 1), (3, 0, 3, 0, 1), (2, 1, 2, 0, 0), (3, 1, 3, 0, 0)]
        a[3, 2] = [(3, 2, 3, 3, 1)]
        a[0, 2] = [(2, 1, 2, 2, 1)]
        a[0, 3] = [(3, 1, 3, 3, 1)]
        b[0, 2] = [(3, 1, 2, 3, 1)]
        b[0, 3] = [(2, 1, 3, 2, 1)]
        b[1, 3] = [(1, 2, 3, 1, 1)]
        order = self.order
        order[0, 1] = [1, 3, 0, 2]
        order[0, 2] = [2, 3, 0, 1]
        order[0, 3] = [3, 2, 0, 1]
        order[1, 2] = [2, 1, 0, 3]
        order[1, 3] = [1, 3, 0, 2]
        order[2, 3] = [2, 0, 3, 1]

    def table(self, get):
        n = self.n
        return [get((i // n, i % n)) for i in range(n * n)]


def xor(a, b, n):
    out, bit = 0, 1
    while bit < n:
        out = out + bit * lax.rem(a // bit + b // bit, 2)
        bit *= 2
    return out


def kernel(
    n_rcv, n_src, mask_ref, piece_ref, refl_ref, focal_ref,
    a_buf, gr, gc, y, acc, focal, slab, arrived,
    load_sem, own_sem, row_send, pass_send, relay_send, gr_recv,
    col_send, down_send, step_send, gc_recv, gc_local, slab_send, slab_recv,
):
    n_dev = n_rcv * n_src
    n = n_src // 2
    plan = Plan(n)
    r = lax.axis_index("rcv")
    s = lax.axis_index("src")
    me = r * n_src + s
    c = s // 2
    h = lax.rem(s, 2)
    chip = r * n + c
    own_p, rows = gr.shape[2], gr.shape[3]
    n_p = own_p * n_src
    cols = gc.shape[3]
    out_rows = n_p // n_dev
    quarter = 2 * own_p
    n_tiles, row_tiles = cols // TILE, rows // TILE
    user = c >= r
    on_diag = c == r
    full = c > r

    def look(get, default=0):
        value = jnp.int32(default)
        for i, entry in enumerate(plan.table(get)):
            if entry != default:
                value = jnp.where(chip == i, entry, value)
        return value

    def width(lists):
        return max([len(ops) for ops in lists.values()] + [0])

    def entry(lists, i, field=None, default=-1):
        def get(key):
            ops = lists.get(key, [])
            if i >= len(ops):
                return default
            return ops[i] if field is None else ops[i][field]

        return get

    def load(t):
        return pltpu.make_async_copy(
            refl_ref.at[:, :, pl.ds(t * TILE, TILE)], a_buf.at[t], load_sem.at[t]
        )

    own_copy = pltpu.make_async_copy(piece_ref, gr.at[h], own_sem)

    @pl.when(user)
    def _():
        own_copy.start()
        for t in range(n_tiles):
            load(t).start()

    barrier = pltpu.get_barrier_semaphore()

    @pl.loop(1, n_dev)
    def _(i):
        other = lax.rem(me + i, n_dev)
        pl.semaphore_signal(
            barrier, inc=1, device_id=(other // n_src, lax.rem(other, n_src)), device_id_type=MESH
        )

    pl.semaphore_wait(barrier, n_dev - 1)

    def row_to(i):
        to = look(entry(plan.row, i))
        slot = 2 * xor(c, to, n) + h
        return to >= 0, pltpu.make_async_remote_copy(
            src_ref=piece_ref, dst_ref=gr.at[slot], send_sem=row_send.at[i], recv_sem=gr_recv.at[slot],
            device_id=(r, 2 * to + h), device_id_type=MESH,
        )

    def to_partner(j):
        slot = 2 * j + h
        src = piece_ref if j == 0 else gr.at[slot]
        return pltpu.make_async_remote_copy(
            src_ref=src, dst_ref=gr.at[slot], send_sem=pass_send.at[j], recv_sem=gr_recv.at[slot],
            device_id=(r, 2 * c + 1 - h), device_id_type=MESH,
        )

    def arrival(slot):
        return pltpu.make_async_remote_copy(
            src_ref=piece_ref, dst_ref=gr.at[slot], send_sem=pass_send.at[0], recv_sem=gr_recv.at[slot],
            device_id=(r, 2 * c + 1 - h), device_id_type=MESH,
        )

    def relay_to(j, i):
        lists = {key[0]: ops for key, ops in plan.relay.items() if key[1] == j}
        to = look(entry(lists, i))
        slot = 2 * j + h
        there = 2 * xor(xor(c, j, n), to, n) + h
        return to >= 0, pltpu.make_async_remote_copy(
            src_ref=gr.at[slot], dst_ref=gr.at[there], send_sem=relay_send.at[j, i],
            recv_sem=gr_recv.at[there], device_id=(r, 2 * to + h), device_id_type=MESH,
        )

    def relays(j):
        return width({key: ops for key, ops in plan.relay.items() if key[1] == j})

    def col_part(ref_slot, half):
        return gc.at[ref_slot, :, pl.ds(pl.multiple_of(half * own_p, own_p), own_p), :]

    def col_to(i, k):
        z = look(entry(plan.col, i, 0))
        to = look(entry(plan.col, i, 1))
        slot = look(entry(plan.col, i, 2))
        return z >= 0, pltpu.make_async_remote_copy(
            src_ref=piece_ref.at[:, :, pl.ds(k * cols, cols)], dst_ref=col_part(slot, h),
            send_sem=col_send.at[i, k], recv_sem=gc_recv.at[2 * slot + h],
            device_id=(z, 2 * to + k), device_id_type=MESH,
        )

    def down_to(j, i, half):
        lists = {key[0]: ops for key, ops in plan.down.items() if key[1] == j}
        z = look(entry(lists, i))
        q = xor(c, j, n)
        return z >= 0, pltpu.make_async_remote_copy(
            src_ref=gr.at[2 * j + half, :, :, pl.ds(pl.multiple_of(h * cols, cols), cols)],
            dst_ref=col_part(q, half), send_sem=down_send.at[j, i, half], recv_sem=gc_recv.at[2 * q + half],
            device_id=(z, s), device_id_type=MESH,
        )

    def downs(j):
        return width({key: ops for key, ops in plan.down.items() if key[1] == j})

    def step_to(stage, i, half):
        lists = plan.passes[stage]
        slot = look(entry(lists, i, 0))
        there = look(entry(lists, i, 3))
        return slot >= 0, look(entry(lists, i, 4)) == 1, slot, pltpu.make_async_remote_copy(
            src_ref=col_part(slot, half), dst_ref=col_part(there, half),
            send_sem=step_send.at[stage, i, half], recv_sem=gc_recv.at[2 * there + half],
            device_id=(look(entry(lists, i, 1)), 2 * look(entry(lists, i, 2)) + h), device_id_type=MESH,
        )

    def col_arrival(slot, half):
        return pltpu.make_async_remote_copy(
            src_ref=piece_ref.at[:, :, pl.ds(0, cols)], dst_ref=col_part(slot, half),
            send_sem=col_send.at[0, 0], recv_sem=gc_recv.at[2 * slot + half],
            device_id=(r, 2 * c + 1 - h), device_id_type=MESH,
        )

    def to_local(j, half):
        q = xor(c, j, n)
        return pltpu.make_async_copy(
            gr.at[2 * j + half, :, :, pl.ds(pl.multiple_of(h * cols, cols), cols)],
            col_part(q, half), gc_local.at[j, half],
        )

    def pass_on(stage):
        for i in range(width(plan.passes[stage])):
            for half in range(2):
                valid, waits, slot, copy = step_to(stage, i, half)

                @pl.when(valid)
                def _():
                    @pl.when(waits)
                    def _():
                        col_arrival(slot, half).wait_recv()

                    copy.start()

    @pl.when(user)
    def _():
        to_partner(0).start()

    for i in range(width(plan.row)):
        valid, copy = row_to(i)
        pl.when(valid)(copy.start)
    for i in range(width(plan.col)):
        for k in range(2):
            valid, copy = col_to(i, k)
            pl.when(valid)(copy.start)

    @pl.when(user)
    def _():
        own_copy.wait()

    def take(j):
        @pl.when(user)
        def _():
            arrival(2 * j + h).wait_recv()
            to_partner(j).start()
            for i in range(relays(j)):
                valid, copy = relay_to(j, i)
                pl.when(valid)(copy.start)

    def twin(j):
        @pl.when(user)
        def _():
            arrival(2 * j + 1 - h).wait_recv()
            for half in range(2):
                for i in range(downs(j)):
                    valid, copy = down_to(j, i, half)
                    pl.when(valid)(copy.start)

                @pl.when(on_diag)
                def _():
                    to_local(j, half).start()

    step_rows = min(rows, 1024)
    step_tiles = step_rows // TILE

    def clean(t, first, count):
        for j in range(first, first + count):
            m = mask_ref[j, t]
            at = pl.ds(j * TILE, TILE)
            for z in range(2):
                tile = a_buf[t, z, at, :]
                a_buf[t, z, at, :] = jnp.where(m == 1, tile, jnp.zeros_like(tile))

    def focal_rows(j, half):
        return pl.ds(pl.multiple_of(xor(c, j, n) * quarter + half * own_p, own_p), own_p)

    def keep(z, t, j0, nj, block):
        at = pl.ds(pl.multiple_of(t * TILE, TILE), TILE)
        block = block.astype(bf16)
        for j in range(nj):
            for half in range(2):
                for part in range(2):
                    start = ((j * 2 + half) * 2 + part) * own_p
                    y[z, part, focal_rows(j0 + j, half), at] = block[start:start + own_p]

    def first(j0, nj):
        m_rows = nj * 2 * quarter

        @pl.when(full)
        def _():
            @pl.loop(0, n_tiles)
            def _(t):
                if j0 == 0:
                    load(t).wait()
                    clean(t, 0, row_tiles)
                left = gr[2 * j0:2 * (j0 + nj)].reshape(m_rows, rows)
                for z in range(2):
                    keep(z, t, j0, nj, dot_nn(left, a_buf[t, z]))

        @pl.when(on_diag)
        def _():
            @pl.loop(0, n_tiles)
            def _(t):
                if j0 == 0:
                    load(t).wait()
                    clean(t, 0, row_tiles)
                col_end = h * cols + (t + 1) * TILE
                for k in range(rows // step_rows):
                    def step():
                        left = gr[2 * j0:2 * (j0 + nj), :, :, k * step_rows:(k + 1) * step_rows]
                        left = left.reshape(m_rows, step_rows)
                        for z in range(2):
                            term = dot_nn(left, a_buf[t, z, k * step_rows:(k + 1) * step_rows, :])
                            if k == 0:
                                acc[z, :m_rows] = term
                            else:
                                acc[z, :m_rows] += term

                    if k == 0:
                        step()
                    else:
                        pl.when(k * step_rows < col_end)(step)
                for z in range(2):
                    keep(z, t, j0, nj, acc[z, :m_rows])

    unit = max(quarter, 128)
    per = unit // quarter

    def second(i, direct, mirror):
        g = jnp.concatenate([gc[i * per + k, part] for part in range(2) for k in range(per)], axis=0)
        here = pl.ds(pl.multiple_of(i * unit, unit), unit)
        sums, turns = [], []
        for z in range(2):
            by_re = dot_nt(y[z, 0], g)
            by_im = dot_nt(y[z, 1], g)
            sums.append(by_re[:, :unit] + by_im[:, unit:])
            turns.append(by_re[:, unit:] - by_im[:, :unit])
        for part in range(2):
            turn = turns[0] if part else -turns[1]
            if direct:
                focal[part, :, here] += sums[part] + turn
            if mirror:
                focal[part, here, :] += (sums[part] - turn).T

    groups = [[0], [1, 2]] + ([list(range(3, n))] if n > 3 else [])
    for stage, group in enumerate(groups):
        if stage:
            for j in group:
                take(j)
        if stage:
            pass_on(stage - 1)
        for j in group:
            twin(j)
        first(group[0], len(group))

    for part in range(2):
        @pl.when(user)
        def _():
            focal[part] = jnp.zeros_like(focal[part])

    @pl.when(full)
    def _():
        @pl.loop(0, n // per)
        def _(i):
            slot = jnp.int32(0)
            waits = jnp.bool_(False)
            for k in range(n // per):
                slot = jnp.where(i == k, look(lambda key: plan.order[key][k]), slot)
                waits = waits | ((i == k) & (look(lambda key: plan.waits[key][k], 1) == 1))

            @pl.when(waits)
            def _():
                for k in range(per):
                    col_arrival(slot * per + k, 0).wait_recv()
                    col_arrival(slot * per + k, 1).wait_recv()

            second(slot, True, True)

    @pl.when(on_diag)
    def _():
        for j in range(n):
            for half in range(2):
                to_local(j, half).wait()

        @pl.loop(0, n // per)
        def _(q):
            second(q, True, False)

        @pl.loop(0, n_tiles)
        def _(t):
            row = h * n_tiles + t
            at_r = pl.ds(pl.multiple_of(row * TILE, TILE), TILE)
            at_c = pl.ds(pl.multiple_of(t * TILE, TILE), TILE)
            left = gr[:, :, :, at_r].reshape(2 * n_p, TILE)
            for z in range(2):
                term = dot_nn(left, a_buf[t, z, at_r, :])
                for j in range(n_src):
                    for part in range(2):
                        at_p = focal_rows(j // 2, j % 2)
                        start = (j * 2 + part) * own_p
                        kept = y[z, part, at_p, at_c].astype(f32) - term[start:start + own_p]
                        y[z, part, at_p, at_c] = kept.astype(bf16)

        @pl.loop(0, n // per)
        def _(q):
            second(q, False, True)

    @pl.when(user)
    def _():
        group = max(16, out_rows)

        @pl.loop(0, n_p // group)
        def _(g):
            at = pl.ds(pl.multiple_of(g * group, group), group)
            for part in range(2):
                block = focal[part, at, :]
                for j in range(group // out_rows):
                    slab[g * (group // out_rows) + j, :, part * n_p:(part + 1) * n_p] = block[
                        j * out_rows:(j + 1) * out_rows
                    ].astype(bf16)

    def slab_to(other):
        return pltpu.make_async_remote_copy(
            src_ref=slab.at[other], dst_ref=arrived.at[me], send_sem=slab_send.at[other],
            recv_sem=slab_recv.at[me],
            device_id=(other // n_src, lax.rem(other, n_src)), device_id_type=MESH,
        )

    def slab_from(other):
        return pltpu.make_async_remote_copy(
            src_ref=slab.at[me], dst_ref=arrived.at[other], send_sem=slab_send.at[other],
            recv_sem=slab_recv.at[other],
            device_id=(other // n_src, lax.rem(other, n_src)), device_id_type=MESH,
        )

    @pl.when(user)
    def _():
        @pl.loop(1, n_dev)
        def _(i):
            slab_to(lax.rem(me + i, n_dev)).start()

    focal_ref[...] = jnp.zeros_like(focal_ref)

    @pl.when(user)
    def _():
        focal_ref[...] = slab[me].astype(f32)

    for other in range(n_dev):
        if (other % n_src) // 2 >= other // n_src:
            @pl.when(me != other)
            def _():
                slab_from(other).wait_recv()
                focal_ref[...] += arrived[other].astype(f32)

    @pl.when(user)
    def _():
        @pl.loop(1, n_dev)
        def _(i):
            slab_to(lax.rem(me + i, n_dev)).wait_send()

    for i in range(width(plan.row)):
        valid, copy = row_to(i)
        pl.when(valid)(copy.wait_send)
    for i in range(width(plan.col)):
        for k in range(2):
            valid, copy = col_to(i, k)
            pl.when(valid)(copy.wait_send)
    for stage in range(len(plan.passes)):
        for i in range(width(plan.passes[stage])):
            for half in range(2):
                valid, _, _, copy = step_to(stage, i, half)
                pl.when(valid)(copy.wait_send)

    @pl.when(user)
    def _():
        for j in range(n):
            to_partner(j).wait_send()
            for i in range(relays(j)):
                valid, copy = relay_to(j, i)
                pl.when(valid)(copy.wait_send)
            for half in range(2):
                for i in range(downs(j)):
                    valid, copy = down_to(j, i, half)
                    pl.when(valid)(copy.wait_send)


def body(reflection, green, tile_mask, reference_index):
    rows, cols = reflection.shape[1], reflection.shape[2]
    n_rcv, n_src = lax.axis_size("rcv"), lax.axis_size("src")
    n_dev = n_rcv * n_src
    own_p = green.shape[2]
    n_p = own_p * n_src
    out_rows = n_p // n_dev
    n = n_src // 2
    assert n == n_rcv and rows == 2 * cols
    r, s = lax.axis_index("rcv"), lax.axis_index("src")
    row_tiles, n_tiles = rows // TILE, cols // TILE
    tile_block = lax.dynamic_slice(tile_mask, (r * row_tiles, s * n_tiles), (row_tiles, n_tiles))
    piece = jnp.swapaxes(green, 1, 2)
    dma = pltpu.SemaphoreType.DMA
    any_spec = pl.BlockSpec(memory_space=pl.ANY)
    focal = pl.pallas_call(
        functools.partial(kernel, n_rcv, n_src),
        out_shape=jax.ShapeDtypeStruct((out_rows, 2 * n_p), f32),
        in_specs=[pl.BlockSpec(memory_space=pltpu.SMEM), any_spec, any_spec],
        out_specs=pl.BlockSpec(memory_space=pltpu.VMEM),
        scratch_shapes=[
            pltpu.VMEM((n_tiles, 2, rows, TILE), bf16),
            pltpu.VMEM((n_src, 2, own_p, rows), bf16),
            pltpu.VMEM((n, 2, 2 * own_p, cols), bf16),
            pltpu.VMEM((2, 2, n_p, cols), bf16),
            pltpu.VMEM((2, 4 * own_p * max(2, n - 3), TILE), f32),
            pltpu.VMEM((2, n_p, n_p), f32),
            pltpu.VMEM((n_dev, out_rows, 2 * n_p), bf16),
            pltpu.VMEM((n_dev, out_rows, 2 * n_p), bf16),
            dma((n_tiles,)), dma, dma((n,)), dma((n,)), dma((n, 2)), dma((n_src,)),
            dma((n, 2)), dma((n, 1, 2)), dma((3, 4, 2)), dma((n_src,)), dma((n, 2)), dma((n_dev,)), dma((n_dev,)),
        ],
        compiler_params=pltpu.CompilerParams(
            collective_id=0, has_side_effects=True, vmem_limit_bytes=63 * 1024 * 1024
        ),
        name="focus",
    )(tile_block, piece, reflection)
    focal_real = focal[:, :n_p]
    focal_imag = focal[:, n_p:]
    chosen = jnp.arange(n_p)[None, :] == reference_index[:, None]
    anchor_real = jnp.sum(jnp.where(chosen, focal_real, 0.0), axis=1)[:, None]
    anchor_imag = jnp.sum(jnp.where(chosen, focal_imag, 0.0), axis=1)[:, None]
    out_real = focal_real * anchor_real + focal_imag * anchor_imag
    out_imag = focal_imag * anchor_real - focal_real * anchor_imag
    return jnp.stack([out_real, out_imag], axis=1)


def solution(mesh):
    return jax.shard_map(
        body,
        mesh=mesh,
        in_specs=(P(None, "rcv", "src"), P(None, "rcv", "src"), P(), P(("rcv", "src"))),
        out_specs=P(("rcv", "src"), None, None),
        check_vma=False,
    )
```

```python
import functools

import jax
import jax.numpy as jnp
from jax import lax
from jax.experimental import pallas as pl
from jax.experimental.pallas import tpu as pltpu
from jax.sharding import PartitionSpec as P

MESH = pl.DeviceIdType.MESH
TILE = 256
f32 = jnp.float32
bf16 = jnp.bfloat16


def dot_nn(a, b):
    return lax.dot_general(a, b, (((1,), (0,)), ((), ())), preferred_element_type=f32)


def dot_nt(a, b):
    return lax.dot_general(a, b, (((1,), (1,)), ((), ())), preferred_element_type=f32)


ROW = [
    {(0, 0): [1, 2], (0, 1): [0, 3], (0, 2): [3, 0], (0, 3): [2, 1], (1, 0): [1, 2], (1, 1): [3], (1, 2): [3], (1, 3): [2, 1], (2, 0): [2, 3], (2, 1): [3, 2], (2, 2): [3], (2, 3): [2], (3, 0): [3], (3, 1): [3], (3, 2): [3]},
    {},
    {},
]
COL = [
    {(1, 0): [(0, 1, 0)], (1, 1): [(0, 1, 1)], (2, 0): [(1, 0, 0)], (2, 1): [(1, 2, 1)], (2, 2): [(0, 2, 2)], (3, 0): [(1, 0, 1), (2, 3, 0)], (3, 1): [(1, 3, 1)], (3, 2): [(2, 3, 2)], (3, 3): [(0, 3, 3), (3, 2, 0)]},
    {},
    {},
]
RELAY = {((0, 1), 2): [0], ((0, 2), 2): [3], ((0, 3), 2): [2], ((0, 3), 1): [1], ((1, 2), 2): [3], ((1, 3), 2): [2], ((1, 3), 1): [1]}
DOWN = {((1, 1), 3): [0], ((1, 1), 2): [0], ((2, 2), 3): [0], ((2, 2), 1): [0], ((3, 3), 2): [0], ((3, 3), 1): [0]}
STEP = [
    {(0, 2): [(2, 1, 2, 2, 1)], (0, 3): [(3, 1, 3, 3, 1)], (1, 0): [(0, 0, 2, 0, 1), (0, 1, 2, 0, 0), (1, 0, 3, 0, 1), (1, 1, 3, 0, 0)], (3, 2): [(0, 2, 3, 3, 1)]},
    {(0, 2): [(3, 1, 2, 3, 1)], (0, 3): [(2, 1, 3, 2, 1)], (1, 3): [(1, 2, 3, 1, 1)]},
    {},
]
ORDER = {(0, 1): [1, 0, 3, 2], (0, 2): [2, 3, 0, 1], (0, 3): [3, 2, 1, 0], (1, 2): [1, 2, 0, 3], (1, 3): [3, 1, 0, 2], (2, 3): [2, 0, 3, 1]}


class Plan:
    def __init__(self, n):
        self.n = n
        self.row, self.col, self.step = ([{}, {}, {}] for _ in range(3))
        self.relay, self.down, self.order = {}, {}, {}
        chips = [(z, c) for z in range(n) for c in range(n)]
        if n == 4:
            for point in range(3):
                self.row[point] = ROW[point]
                self.col[point] = COL[point]
                self.step[point] = STEP[point]
            self.relay, self.down, self.order = RELAY, DOWN, ORDER
        else:
            for z, c in chips:
                self.row[0][z, c] = [t for t in sorted(range(z, n), key=lambda t: t ^ c) if t != c]
                self.col[0][z, c] = [(t, z, c) for t in range(z)]
        waited = {chip: {op[0] for stage in self.step for op in stage.get(chip, []) if op[4]} for chip in chips}
        order = {chip: self.order.get(chip, list(range(n))) for chip in chips}
        self.order = order
        self.waits = {chip: [int(q not in waited[chip]) for q in order[chip]] for chip in chips}

    def table(self, get):
        n = self.n
        return [get((i // n, i % n)) for i in range(n * n)]


def xor(a, b, n):
    out, bit = 0, 1
    while bit < n:
        out = out + bit * lax.rem(a // bit + b // bit, 2)
        bit *= 2
    return out


def kernel(
    n_rcv, n_src, mask_ref, piece_ref, refl_ref, focal_ref,
    a_buf, gr, gc, y, acc, focal, slab, pair, arrived,
    load_sem, own_sem, row_send, pass_send, relay_send, gr_recv,
    col_send, down_send, step_send, gc_recv, gc_local, slab_send, slab_recv,
    pair_send, pair_recv,
):
    n_dev = n_rcv * n_src
    n = n_src // 2
    plan = Plan(n)
    r = lax.axis_index("rcv")
    s = lax.axis_index("src")
    me = r * n_src + s
    c = s // 2
    h = lax.rem(s, 2)
    chip = r * n + c
    own_p, rows = gr.shape[2], gr.shape[3]
    n_p = own_p * n_src
    cols = gc.shape[3]
    out_rows = n_p // n_dev
    quarter = 2 * own_p
    n_tiles, row_tiles = cols // TILE, rows // TILE
    user = c >= r
    on_diag = c == r
    full = c > r

    def look(get, default=0):
        value = jnp.int32(default)
        for i, entry in enumerate(plan.table(get)):
            if entry != default:
                value = jnp.where(chip == i, entry, value)
        return value

    def width(lists):
        return max([len(ops) for ops in lists.values()] + [0])

    def entry(lists, i, field=None, default=-1):
        def get(key):
            ops = lists.get(key, [])
            if i >= len(ops):
                return default
            return ops[i] if field is None else ops[i][field]

        return get

    def load(t):
        return pltpu.make_async_copy(
            refl_ref.at[:, :, pl.ds(t * TILE, TILE)], a_buf.at[t], load_sem.at[t]
        )

    own_copy = pltpu.make_async_copy(piece_ref, gr.at[h], own_sem)

    @pl.when(user)
    def _():
        own_copy.start()
        for t in range(n_tiles):
            load(t).start()

    barrier = pltpu.get_barrier_semaphore()

    @pl.loop(1, n_dev)
    def _(i):
        other = lax.rem(me + i, n_dev)
        pl.semaphore_signal(
            barrier, inc=1, device_id=(other // n_src, lax.rem(other, n_src)), device_id_type=MESH
        )

    pl.semaphore_wait(barrier, n_dev - 1)

    def row_to(point, i):
        to = look(entry(plan.row[point], i))
        slot = 2 * xor(c, to, n) + h
        return to >= 0, pltpu.make_async_remote_copy(
            src_ref=piece_ref, dst_ref=gr.at[slot], send_sem=row_send.at[point, i], recv_sem=gr_recv.at[slot],
            device_id=(r, 2 * to + h), device_id_type=MESH,
        )

    def to_partner(j):
        slot = 2 * j + h
        src = piece_ref if j == 0 else gr.at[slot]
        return pltpu.make_async_remote_copy(
            src_ref=src, dst_ref=gr.at[slot], send_sem=pass_send.at[j], recv_sem=gr_recv.at[slot],
            device_id=(r, 2 * c + 1 - h), device_id_type=MESH,
        )

    def arrival(slot):
        return pltpu.make_async_remote_copy(
            src_ref=piece_ref, dst_ref=gr.at[slot], send_sem=pass_send.at[0], recv_sem=gr_recv.at[slot],
            device_id=(r, 2 * c + 1 - h), device_id_type=MESH,
        )

    def relay_to(j, i):
        lists = {key[0]: ops for key, ops in plan.relay.items() if key[1] == j}
        to = look(entry(lists, i))
        slot = 2 * j + h
        there = 2 * xor(xor(c, j, n), to, n) + h
        return to >= 0, pltpu.make_async_remote_copy(
            src_ref=gr.at[slot], dst_ref=gr.at[there], send_sem=relay_send.at[j, i],
            recv_sem=gr_recv.at[there], device_id=(r, 2 * to + h), device_id_type=MESH,
        )

    def relays(j):
        return width({key: ops for key, ops in plan.relay.items() if key[1] == j})

    def col_part(ref_slot, half):
        return gc.at[ref_slot, :, pl.ds(pl.multiple_of(half * own_p, own_p), own_p), :]

    def col_to(point, i, k):
        lists = plan.col[point]
        z = look(entry(lists, i, 0))
        to = look(entry(lists, i, 1))
        slot = look(entry(lists, i, 2))
        return z >= 0, pltpu.make_async_remote_copy(
            src_ref=piece_ref.at[:, :, pl.ds(k * cols, cols)], dst_ref=col_part(slot, h),
            send_sem=col_send.at[point, i, k], recv_sem=gc_recv.at[2 * slot + h],
            device_id=(z, 2 * to + k), device_id_type=MESH,
        )

    def down_to(j, i, half):
        lists = {key[0]: ops for key, ops in plan.down.items() if key[1] == j}
        z = look(entry(lists, i))
        q = xor(c, j, n)
        return z >= 0, pltpu.make_async_remote_copy(
            src_ref=gr.at[2 * j + half, :, :, pl.ds(pl.multiple_of(h * cols, cols), cols)],
            dst_ref=col_part(q, half), send_sem=down_send.at[j, i, half], recv_sem=gc_recv.at[2 * q + half],
            device_id=(z, s), device_id_type=MESH,
        )

    def downs(j):
        return width({key: ops for key, ops in plan.down.items() if key[1] == j})

    def step_to(stage, i, half):
        lists = plan.step[stage]
        slot = look(entry(lists, i, 0))
        there = look(entry(lists, i, 3))
        return slot >= 0, look(entry(lists, i, 4)) == 1, slot, pltpu.make_async_remote_copy(
            src_ref=col_part(slot, half), dst_ref=col_part(there, half),
            send_sem=step_send.at[stage, i, half], recv_sem=gc_recv.at[2 * there + half],
            device_id=(look(entry(lists, i, 1)), 2 * look(entry(lists, i, 2)) + h), device_id_type=MESH,
        )

    def col_arrival(slot, half):
        return pltpu.make_async_remote_copy(
            src_ref=piece_ref.at[:, :, pl.ds(0, cols)], dst_ref=col_part(slot, half),
            send_sem=col_send.at[0, 0, 0], recv_sem=gc_recv.at[2 * slot + half],
            device_id=(r, 2 * c + 1 - h), device_id_type=MESH,
        )

    def to_local(j, half):
        q = xor(c, j, n)
        return pltpu.make_async_copy(
            gr.at[2 * j + half, :, :, pl.ds(pl.multiple_of(h * cols, cols), cols)],
            col_part(q, half), gc_local.at[j, half],
        )

    def pass_on(stage):
        for i in range(width(plan.step[stage])):
            for half in range(2):
                valid, waits, slot, copy = step_to(stage, i, half)

                @pl.when(valid)
                def _():
                    @pl.when(waits)
                    def _():
                        col_arrival(slot, half).wait_recv()

                    copy.start()

    @pl.when(user)
    def _():
        to_partner(0).start()

    def own_sends(point):
        ops = [row_to(point, i) for i in range(width(plan.row[point]))]
        return ops + [col_to(point, i, k) for i in range(width(plan.col[point])) for k in range(2)]

    def begin(point):
        for valid, copy in own_sends(point):
            pl.when(valid)(copy.start)

    def drained(point):
        later = plan.row[point + 1], plan.col[point + 1]
        return look(lambda chip: int(chip[1] < chip[0] and any(lists.get(chip) for lists in later))) == 1

    begin(0)

    @pl.when(user)
    def _():
        own_copy.wait()

    def take(j):
        arrival(2 * j + h).wait_recv()
        to_partner(j).start()
        for i in range(relays(j)):
            valid, copy = relay_to(j, i)
            pl.when(valid)(copy.start)

    def twin(j):
        arrival(2 * j + 1 - h).wait_recv()
        for half in range(2):
            for i in range(downs(j)):
                valid, copy = down_to(j, i, half)
                pl.when(valid)(copy.start)

            @pl.when(on_diag)
            def _():
                to_local(j, half).start()

    step_rows = min(rows, 1024)
    step_tiles = step_rows // TILE

    def clean(t, first, count):
        for j in range(first, first + count):
            m = mask_ref[j, t]
            at = pl.ds(j * TILE, TILE)
            for z in range(2):
                tile = a_buf[t, z, at, :]
                a_buf[t, z, at, :] = jnp.where(m == 1, tile, jnp.zeros_like(tile))

    def focal_rows(j, half):
        return pl.ds(pl.multiple_of(xor(c, j, n) * quarter + half * own_p, own_p), own_p)

    def keep(z, t, j0, nj, block):
        at = pl.ds(pl.multiple_of(t * TILE, TILE), TILE)
        block = block.astype(bf16)
        for j in range(nj):
            for half in range(2):
                for part in range(2):
                    start = ((j * 2 + half) * 2 + part) * own_p
                    y[z, part, focal_rows(j0 + j, half), at] = block[start:start + own_p]

    def first(j0, nj):
        m_rows = nj * 2 * quarter

        @pl.when(full)
        def _():
            @pl.loop(0, n_tiles)
            def _(t):
                if j0 == 0:
                    load(t).wait()
                    clean(t, 0, row_tiles)
                left = gr[2 * j0:2 * (j0 + nj)].reshape(m_rows, rows)
                for z in range(2):
                    keep(z, t, j0, nj, dot_nn(left, a_buf[t, z]))

        @pl.when(on_diag)
        def _():
            @pl.loop(0, n_tiles)
            def _(t):
                if j0 == 0:
                    load(t).wait()
                    clean(t, 0, row_tiles)
                col_end = h * cols + (t + 1) * TILE
                for k in range(rows // step_rows):
                    def step():
                        left = gr[2 * j0:2 * (j0 + nj), :, :, k * step_rows:(k + 1) * step_rows]
                        left = left.reshape(m_rows, step_rows)
                        for z in range(2):
                            term = dot_nn(left, a_buf[t, z, k * step_rows:(k + 1) * step_rows, :])
                            if k == 0:
                                acc[z, :m_rows] = term
                            else:
                                acc[z, :m_rows] += term

                    if k == 0:
                        step()
                    else:
                        pl.when(k * step_rows < col_end)(step)
                for z in range(2):
                    keep(z, t, j0, nj, acc[z, :m_rows])

    unit = max(quarter, 128)
    per = unit // quarter

    def second(i, direct, mirror):
        g = jnp.concatenate([gc[i * per + k, part] for part in range(2) for k in range(per)], axis=0)
        here = pl.ds(pl.multiple_of(i * unit, unit), unit)
        sums, turns = [], []
        for z in range(2):
            by_re = dot_nt(y[z, 0], g)
            by_im = dot_nt(y[z, 1], g)
            sums.append(by_re[:, :unit] + by_im[:, unit:])
            turns.append(by_re[:, unit:] - by_im[:, :unit])
        for part in range(2):
            turn = turns[0] if part else -turns[1]
            if direct:
                focal[part, :, here] += sums[part] + turn
            if mirror:
                focal[part, here, :] += (sums[part] - turn).T

    groups = [[0], [1, 2]] + ([list(range(3, n))] if n > 3 else [])
    for stage, group in enumerate(groups):
        if stage:
            for j in group:
                pl.when(user)(functools.partial(take, j))
                pl.when(on_diag)(functools.partial(twin, j))
            for valid, copy in own_sends(stage - 1):
                pl.when(valid & drained(stage - 1))(copy.wait_send)
            begin(stage)
            pass_on(stage - 1)
        for j in group:
            pl.when(full if stage else user)(functools.partial(twin, j))
        first(group[0], len(group))
    pass_on(2)

    for part in range(2):
        @pl.when(user)
        def _():
            focal[part] = jnp.zeros_like(focal[part])

    @pl.when(full)
    def _():
        @pl.loop(0, n // per)
        def _(i):
            slot = jnp.int32(0)
            waits = jnp.bool_(False)
            for k in range(n // per):
                slot = jnp.where(i == k, look(lambda key: plan.order[key][k]), slot)
                waits = waits | ((i == k) & (look(lambda key: plan.waits[key][k], 1) == 1))

            @pl.when(waits)
            def _():
                for k in range(per):
                    col_arrival(slot * per + k, 0).wait_recv()
                    col_arrival(slot * per + k, 1).wait_recv()

            second(slot, True, True)

    @pl.when(on_diag)
    def _():
        for j in range(n):
            for half in range(2):
                to_local(j, half).wait()

        @pl.loop(0, n // per)
        def _(q):
            second(q, True, False)

        @pl.loop(0, n_tiles)
        def _(t):
            row = h * n_tiles + t
            at_r = pl.ds(pl.multiple_of(row * TILE, TILE), TILE)
            at_c = pl.ds(pl.multiple_of(t * TILE, TILE), TILE)
            left = gr[:, :, :, at_r].reshape(2 * n_p, TILE)
            for z in range(2):
                term = dot_nn(left, a_buf[t, z, at_r, :])
                for j in range(n_src):
                    for part in range(2):
                        at_p = focal_rows(j // 2, j % 2)
                        start = (j * 2 + part) * own_p
                        kept = y[z, part, at_p, at_c].astype(f32) - term[start:start + own_p]
                        y[z, part, at_p, at_c] = kept.astype(bf16)

        @pl.loop(0, n // per)
        def _(q):
            second(q, False, True)

    share = n_dev // 2
    group = max(16, out_rows)
    each = group // out_rows
    n_groups = n_p // group // 2

    def rows_of(half, g):
        return pl.ds(pl.multiple_of((half * n_groups + g) * group, group), group)

    def slab_pair(start):
        return pltpu.make_async_remote_copy(
            src_ref=slab.at[pl.ds(start, share)], dst_ref=pair, send_sem=pair_send, recv_sem=pair_recv,
            device_id=(r, 2 * c + 1 - h), device_id_type=MESH,
        )

    def slab_to(i):
        other = h * share + i
        return pltpu.make_async_remote_copy(
            src_ref=slab.at[other], dst_ref=arrived.at[chip], send_sem=slab_send.at[i],
            recv_sem=slab_recv.at[chip],
            device_id=(other // n_src, lax.rem(other, n_src)), device_id_type=MESH,
        )

    def slab_from(z, b):
        return pltpu.make_async_remote_copy(
            src_ref=slab.at[0], dst_ref=arrived.at[z * n + b], send_sem=slab_send.at[0],
            recv_sem=slab_recv.at[z * n + b], device_id=(z, 2 * b + me // share), device_id_type=MESH,
        )

    @pl.when(user)
    def _():
        @pl.loop(0, n_groups)
        def _(g):
            for part in range(2):
                block = focal[part, rows_of(1 - h, g), :]
                for j in range(each):
                    slab[(1 - h) * share + g * each + j, :, part * n_p:(part + 1) * n_p] = block[
                        j * out_rows:(j + 1) * out_rows
                    ].astype(bf16)

        slab_pair((1 - h) * share).start()
        slab_pair(0).wait_recv()

        def begin_slab(i):
            @pl.when(h * share + i != me)
            def _():
                slab_to(i).start()

        @pl.loop(0, n_groups)
        def _(g):
            for part in range(2):
                block = focal[part, rows_of(h, g), :]
                for j in range(each):
                    at = slice(part * n_p, (part + 1) * n_p)
                    slab[h * share + g * each + j, :, at] = (
                        block[j * out_rows:(j + 1) * out_rows] + pair[g * each + j, :, at].astype(f32)
                    ).astype(bf16)

            @pl.when(g > 0)
            def _():
                for j in range(each):
                    begin_slab((g - 1) * each + j)

        for j in range(each):
            begin_slab(share - each + j)

    focal_ref[...] = jnp.zeros_like(focal_ref)
    own_half = h == me // share

    @pl.when(user & own_half)
    def _():
        focal_ref[...] = slab[me].astype(f32)

    for z in range(n):
        for b in range(z, n):
            @pl.when(jnp.logical_not(own_half & (chip == z * n + b)))
            def _():
                slab_from(z, b).wait_recv()
                focal_ref[...] += arrived[z * n + b].astype(f32)

    @pl.when(user)
    def _():
        slab_pair((1 - h) * share).wait_send()

        @pl.loop(0, share)
        def _(i):
            @pl.when(h * share + i != me)
            def _():
                slab_to(i).wait_send()

    for point in range(3):
        for valid, copy in own_sends(point):
            if point < 2:
                valid = valid & jnp.logical_not(drained(point))
            pl.when(valid)(copy.wait_send)
    for stage in range(3):
        for i in range(width(plan.step[stage])):
            for half in range(2):
                valid, _, _, copy = step_to(stage, i, half)
                pl.when(valid)(copy.wait_send)

    @pl.when(user)
    def _():
        for j in range(n):
            to_partner(j).wait_send()
            for i in range(relays(j)):
                valid, copy = relay_to(j, i)
                pl.when(valid)(copy.wait_send)
            for half in range(2):
                for i in range(downs(j)):
                    valid, copy = down_to(j, i, half)
                    pl.when(valid)(copy.wait_send)


def body(reflection, green, tile_mask, reference_index):
    rows, cols = reflection.shape[1], reflection.shape[2]
    n_rcv, n_src = lax.axis_size("rcv"), lax.axis_size("src")
    n_dev = n_rcv * n_src
    own_p = green.shape[2]
    n_p = own_p * n_src
    out_rows = n_p // n_dev
    n = n_src // 2
    assert n == n_rcv and rows == 2 * cols
    r, s = lax.axis_index("rcv"), lax.axis_index("src")
    row_tiles, n_tiles = rows // TILE, cols // TILE
    tile_block = lax.dynamic_slice(tile_mask, (r * row_tiles, s * n_tiles), (row_tiles, n_tiles))
    piece = jnp.swapaxes(green, 1, 2)
    dma = pltpu.SemaphoreType.DMA
    any_spec = pl.BlockSpec(memory_space=pl.ANY)
    focal = pl.pallas_call(
        functools.partial(kernel, n_rcv, n_src),
        out_shape=jax.ShapeDtypeStruct((out_rows, 2 * n_p), f32),
        in_specs=[pl.BlockSpec(memory_space=pltpu.SMEM), any_spec, any_spec],
        out_specs=pl.BlockSpec(memory_space=pltpu.VMEM),
        scratch_shapes=[
            pltpu.VMEM((n_tiles, 2, rows, TILE), bf16),
            pltpu.VMEM((n_src, 2, own_p, rows), bf16),
            pltpu.VMEM((n, 2, 2 * own_p, cols), bf16),
            pltpu.VMEM((2, 2, n_p, cols), bf16),
            pltpu.VMEM((2, 4 * own_p * max(2, n - 3), TILE), f32),
            pltpu.VMEM((2, n_p, n_p), f32),
            pltpu.VMEM((n_dev, out_rows, 2 * n_p), bf16),
            pltpu.VMEM((n_dev // 2, out_rows, 2 * n_p), bf16),
            pltpu.VMEM((n_dev // 2, out_rows, 2 * n_p), bf16),
            dma((n_tiles,)), dma, dma((3, n)), dma((n,)), dma((n, n)), dma((n_src,)),
            dma((3, 2 * n, 2)), dma((n, n, 2)), dma((3, 2 * n, 2)), dma((n_src,)), dma((n, 2)), dma((n_dev // 2,)), dma((n_dev // 2,)),
            dma, dma,
        ],
        compiler_params=pltpu.CompilerParams(
            collective_id=0, has_side_effects=True, vmem_limit_bytes=63 * 1024 * 1024
        ),
        name="focus",
    )(tile_block, piece, reflection)
    focal_real = focal[:, :n_p]
    focal_imag = focal[:, n_p:]
    chosen = jnp.arange(n_p)[None, :] == reference_index[:, None]
    anchor_real = jnp.sum(jnp.where(chosen, focal_real, 0.0), axis=1)[:, None]
    anchor_imag = jnp.sum(jnp.where(chosen, focal_imag, 0.0), axis=1)[:, None]
    out_real = focal_real * anchor_real + focal_imag * anchor_imag
    out_imag = focal_imag * anchor_real - focal_real * anchor_imag
    return jnp.stack([out_real, out_imag], axis=1)


def solution(mesh):
    return jax.shard_map(
        body,
        mesh=mesh,
        in_specs=(P(None, "rcv", "src"), P(None, "rcv", "src"), P(), P(("rcv", "src"))),
        out_specs=P(("rcv", "src"), None, None),
        check_vma=False,
    )
```

```python
import functools

import jax
import jax.numpy as jnp
from jax import lax
from jax.experimental import pallas as pl
from jax.experimental.pallas import tpu as pltpu
from jax.sharding import PartitionSpec as P

MESH = pl.DeviceIdType.MESH
TILE = 256
f32 = jnp.float32
bf16 = jnp.bfloat16


def dot_nn(a, b):
    return lax.dot_general(a, b, (((1,), (0,)), ((), ())), preferred_element_type=f32)


def dot_nt(a, b):
    return lax.dot_general(a, b, (((1,), (1,)), ((), ())), preferred_element_type=f32)


ROW = [
    {(0, 0): [1, 2], (0, 1): [0, 3], (0, 2): [3, 0], (0, 3): [2, 1], (1, 0): [1, 2], (1, 1): [3], (1, 2): [3], (1, 3): [2, 1], (2, 0): [2, 3], (2, 1): [3, 2], (2, 2): [3], (2, 3): [2], (3, 0): [3], (3, 1): [3], (3, 2): [3]},
    {},
    {},
]
COL = [
    {(1, 1): [(0, 1, 1)], (2, 0): [(1, 0, 0)], (2, 2): [(0, 2, 2)], (3, 0): [(1, 0, 1)], (3, 3): [(0, 3, 3), (3, 2, 0)]},
    {(1, 0): [(0, 1, 0)], (2, 1): [(1, 2, 1)], (3, 0): [(2, 3, 0)], (3, 1): [(1, 3, 1)], (3, 2): [(2, 3, 2)]},
    {},
]
RELAY = {((0, 1), 2): [0], ((0, 2), 2): [3], ((0, 3), 2): [2], ((0, 3), 1): [1], ((1, 2), 2): [3], ((1, 3), 2): [2], ((1, 3), 1): [1]}
DOWN = {((1, 1), 3): [0], ((1, 1), 2): [0], ((2, 2), 3): [0], ((2, 2), 1): [0], ((3, 3), 2): [0], ((3, 3), 1): [0]}
STEP = [
    {(0, 2): [(2, 1, 2, 2, 1)], (0, 3): [(3, 1, 3, 3, 1)], (1, 0): [(0, 0, 2, 0, 1), (0, 1, 2, 0, 0), (1, 0, 3, 0, 1), (1, 1, 3, 0, 0)], (3, 2): [(0, 2, 3, 3, 1)]},
    {(0, 2): [(3, 1, 2, 3, 1)], (0, 3): [(2, 1, 3, 2, 1)], (1, 3): [(1, 2, 3, 1, 1)]},
    {},
]
ORDER = {(0, 1): [1, 3, 2, 0], (0, 2): [2, 3, 0, 1], (0, 3): [3, 2, 1, 0], (1, 2): [2, 0, 3, 1], (1, 3): [3, 0, 2, 1], (2, 3): [3, 0, 2, 1]}
EARLY = [(0, 0), (2, 2), (3, 3)]


class Plan:
    def __init__(self, n):
        self.n = n
        self.row, self.col, self.step = ([{}, {}, {}] for _ in range(3))
        self.relay, self.down, self.order = {}, {}, {}
        self.early = []
        chips = [(z, c) for z in range(n) for c in range(n)]
        if n == 4:
            for point in range(3):
                self.row[point] = ROW[point]
                self.col[point] = COL[point]
                self.step[point] = STEP[point]
            self.relay, self.down, self.order, self.early = RELAY, DOWN, ORDER, EARLY
        else:
            for z, c in chips:
                self.row[0][z, c] = [t for t in sorted(range(z, n), key=lambda t: t ^ c) if t != c]
                self.col[0][z, c] = [(t, z, c) for t in range(z)]
        waited = {chip: {op[0] for stage in self.step for op in stage.get(chip, []) if op[4]} for chip in chips}
        order = {chip: self.order.get(chip, list(range(n))) for chip in chips}
        self.order = order
        self.waits = {chip: [int(q not in waited[chip]) for q in order[chip]] for chip in chips}

    def table(self, get):
        n = self.n
        return [get((i // n, i % n)) for i in range(n * n)]


def xor(a, b, n):
    out, bit = 0, 1
    while bit < n:
        out = out + bit * lax.rem(a // bit + b // bit, 2)
        bit *= 2
    return out


def kernel(
    n_rcv, n_src, mask_ref, index_ref, piece_ref, refl_ref, out_ref,
    focal_ref, a_buf, d_buf, gr, gc, y, y_diag, acc, focal, slab, pair, arrived,
    load_sem, own_sem, row_send, pass_send, relay_send, gr_recv,
    col_send, down_send, step_send, gc_recv, gc_local, slab_send, slab_recv,
    pair_send, pair_recv,
):
    n_dev = n_rcv * n_src
    n = n_src // 2
    plan = Plan(n)
    r = lax.axis_index("rcv")
    s = lax.axis_index("src")
    me = r * n_src + s
    c = s // 2
    h = lax.rem(s, 2)
    chip = r * n + c
    own_p, rows = gr.shape[2], gr.shape[3]
    n_p = own_p * n_src
    cols = gc.shape[3]
    out_rows = n_p // n_dev
    quarter = 2 * own_p
    n_tiles, row_tiles = cols // TILE, rows // TILE
    user = c >= r
    on_diag = c == r
    full = c > r

    def look(get, default=0):
        value = jnp.int32(default)
        for i, entry in enumerate(plan.table(get)):
            if entry != default:
                value = jnp.where(chip == i, entry, value)
        return value

    def width(lists):
        return max([len(ops) for ops in lists.values()] + [0])

    def entry(lists, i, field=None, default=-1):
        def get(key):
            ops = lists.get(key, [])
            if i >= len(ops):
                return default
            return ops[i] if field is None else ops[i][field]

        return get

    def load(t):
        return pltpu.make_async_copy(
            refl_ref.at[:, :, pl.ds(t * TILE, TILE)], a_buf.at[t], load_sem.at[t]
        )

    own_copy = pltpu.make_async_copy(piece_ref, gr.at[h], own_sem)

    @pl.when(user)
    def _():
        own_copy.start()
        for t in range(n_tiles):
            load(t).start()

    barrier = pltpu.get_barrier_semaphore()

    @pl.loop(1, n_dev)
    def _(i):
        other = lax.rem(me + i, n_dev)
        pl.semaphore_signal(
            barrier, inc=1, device_id=(other // n_src, lax.rem(other, n_src)), device_id_type=MESH
        )

    pl.semaphore_wait(barrier, n_dev - 1)

    def row_to(point, i):
        to = look(entry(plan.row[point], i))
        slot = 2 * xor(c, to, n) + h
        return to >= 0, pltpu.make_async_remote_copy(
            src_ref=piece_ref, dst_ref=gr.at[slot], send_sem=row_send.at[point, i], recv_sem=gr_recv.at[slot],
            device_id=(r, 2 * to + h), device_id_type=MESH,
        )

    def to_partner(j):
        slot = 2 * j + h
        src = piece_ref if j == 0 else gr.at[slot]
        return pltpu.make_async_remote_copy(
            src_ref=src, dst_ref=gr.at[slot], send_sem=pass_send.at[j], recv_sem=gr_recv.at[slot],
            device_id=(r, 2 * c + 1 - h), device_id_type=MESH,
        )

    def arrival(slot):
        return pltpu.make_async_remote_copy(
            src_ref=piece_ref, dst_ref=gr.at[slot], send_sem=pass_send.at[0], recv_sem=gr_recv.at[slot],
            device_id=(r, 2 * c + 1 - h), device_id_type=MESH,
        )

    def relay_to(j, i):
        lists = {key[0]: ops for key, ops in plan.relay.items() if key[1] == j}
        to = look(entry(lists, i))
        slot = 2 * j + h
        there = 2 * xor(xor(c, j, n), to, n) + h
        return to >= 0, pltpu.make_async_remote_copy(
            src_ref=gr.at[slot], dst_ref=gr.at[there], send_sem=relay_send.at[j, i],
            recv_sem=gr_recv.at[there], device_id=(r, 2 * to + h), device_id_type=MESH,
        )

    def relays(j):
        return width({key: ops for key, ops in plan.relay.items() if key[1] == j})

    def col_part(ref_slot, half):
        return gc.at[ref_slot, :, pl.ds(pl.multiple_of(half * own_p, own_p), own_p), :]

    def col_to(point, i, k):
        lists = plan.col[point]
        z = look(entry(lists, i, 0))
        to = look(entry(lists, i, 1))
        slot = look(entry(lists, i, 2))
        return z >= 0, pltpu.make_async_remote_copy(
            src_ref=piece_ref.at[:, :, pl.ds(k * cols, cols)], dst_ref=col_part(slot, h),
            send_sem=col_send.at[point, i, k], recv_sem=gc_recv.at[2 * slot + h],
            device_id=(z, 2 * to + k), device_id_type=MESH,
        )

    def down_to(j, i, half):
        lists = {key[0]: ops for key, ops in plan.down.items() if key[1] == j}
        z = look(entry(lists, i))
        q = xor(c, j, n)
        return z >= 0, pltpu.make_async_remote_copy(
            src_ref=gr.at[2 * j + half, :, :, pl.ds(pl.multiple_of(h * cols, cols), cols)],
            dst_ref=col_part(q, half), send_sem=down_send.at[j, i, half], recv_sem=gc_recv.at[2 * q + half],
            device_id=(z, s), device_id_type=MESH,
        )

    def downs(j):
        return width({key: ops for key, ops in plan.down.items() if key[1] == j})

    def step_to(stage, i, half):
        lists = plan.step[stage]
        slot = look(entry(lists, i, 0))
        there = look(entry(lists, i, 3))
        return slot >= 0, look(entry(lists, i, 4)) == 1, slot, pltpu.make_async_remote_copy(
            src_ref=col_part(slot, half), dst_ref=col_part(there, half),
            send_sem=step_send.at[stage, i, half], recv_sem=gc_recv.at[2 * there + half],
            device_id=(look(entry(lists, i, 1)), 2 * look(entry(lists, i, 2)) + h), device_id_type=MESH,
        )

    def col_arrival(slot, half):
        return pltpu.make_async_remote_copy(
            src_ref=piece_ref.at[:, :, pl.ds(0, cols)], dst_ref=col_part(slot, half),
            send_sem=col_send.at[0, 0, 0], recv_sem=gc_recv.at[2 * slot + half],
            device_id=(r, 2 * c + 1 - h), device_id_type=MESH,
        )

    def to_local(j, half):
        q = xor(c, j, n)
        return pltpu.make_async_copy(
            gr.at[2 * j + half, :, :, pl.ds(pl.multiple_of(h * cols, cols), cols)],
            col_part(q, half), gc_local.at[j, half],
        )

    def pass_on(stage):
        for i in range(width(plan.step[stage])):
            for half in range(2):
                valid, waits, slot, copy = step_to(stage, i, half)

                @pl.when(valid)
                def _():
                    @pl.when(waits)
                    def _():
                        col_arrival(slot, half).wait_recv()

                    copy.start()

    @pl.when(user)
    def _():
        to_partner(0).start()

    def own_sends(point):
        ops = [row_to(point, i) for i in range(width(plan.row[point]))]
        return ops + [col_to(point, i, k) for i in range(width(plan.col[point])) for k in range(2)]

    def begin(point):
        for valid, copy in own_sends(point):
            pl.when(valid)(copy.start)

    def drained(point):
        later = plan.row[point + 1], plan.col[point + 1]
        return look(lambda chip: int(chip[1] < chip[0] and any(lists.get(chip) for lists in later))) == 1

    begin(0)

    @pl.when(user)
    def _():
        own_copy.wait()

    def take(j):
        arrival(2 * j + h).wait_recv()
        to_partner(j).start()
        for i in range(relays(j)):
            valid, copy = relay_to(j, i)
            pl.when(valid)(copy.start)

    def twin(j):
        arrival(2 * j + 1 - h).wait_recv()
        for half in range(2):
            for i in range(downs(j)):
                valid, copy = down_to(j, i, half)
                pl.when(valid)(copy.start)

            @pl.when(on_diag)
            def _():
                to_local(j, half).start()

    step_rows = min(rows, 1024)
    step_tiles = step_rows // TILE

    def clean(t):
        @pl.when(on_diag)
        def _():
            at = pl.ds(pl.multiple_of((h * n_tiles + t) * TILE, TILE), TILE)
            m = mask_ref[(r * row_tiles + h * n_tiles) + t, s * n_tiles + t]
            for z in range(2):
                tile = a_buf[t, z, at, :]
                d_buf[t, z] = jnp.where(m == 1, tile, jnp.zeros_like(tile))
                a_buf[t, z, at, :] = jnp.zeros_like(tile)

        for j in range(row_tiles):
            m = mask_ref[r * row_tiles + j, s * n_tiles + t]
            at = pl.ds(j * TILE, TILE)
            for z in range(2):
                tile = a_buf[t, z, at, :]
                a_buf[t, z, at, :] = jnp.where(m == 1, tile, jnp.zeros_like(tile))

    unit = max(quarter, 128)
    per = unit // quarter
    n_units = n // per

    def keep(ref, j, z, at, block, start):
        block = block.astype(bf16)
        inner = xor(c, j, n) % per if per > 1 else 0
        for half in range(2):
            for part in range(2):
                begin = start + (half * 2 + part) * own_p
                rows_at = pl.ds(pl.multiple_of(inner * quarter + half * own_p, own_p), own_p)
                ref[z, part, rows_at, at] = block[begin:begin + own_p]

    def columns(t):
        return pl.ds(pl.multiple_of(t * TILE, TILE), TILE)

    def keep_all(z, t, j0, nj, block):
        for j in range(nj):
            keep(y.at[(j0 + j) // per], j0 + j, z, columns(t), block, j * 2 * quarter)

    def first(j0, nj):
        m_rows = nj * 2 * quarter

        @pl.when(full)
        def _():
            @pl.loop(0, n_tiles)
            def _(t):
                if j0 == 0:
                    load(t).wait()
                    clean(t)
                left = gr[2 * j0:2 * (j0 + nj)].reshape(m_rows, rows)
                for z in range(2):
                    keep_all(z, t, j0, nj, dot_nn(left, a_buf[t, z]))

    def first_diag(j0, nj):
        m_rows = nj * 2 * quarter

        @pl.when(on_diag)
        def _():
            @pl.loop(0, n_tiles)
            def _(t):
                if j0 == 0:
                    load(t).wait()
                    clean(t)
                col_end = h * cols + (t + 1) * TILE
                for k in range(rows // step_rows):
                    def step():
                        left = gr[2 * j0:2 * (j0 + nj), :, :, k * step_rows:(k + 1) * step_rows]
                        left = left.reshape(m_rows, step_rows)
                        for z in range(2):
                            term = dot_nn(left, a_buf[t, z, k * step_rows:(k + 1) * step_rows, :])
                            if k == 0:
                                acc[z, :m_rows] = term
                            else:
                                acc[z, :m_rows] += term

                    if k == 0:
                        step()
                    else:
                        pl.when(k * step_rows < col_end)(step)
                for z in range(2):
                    keep_all(z, t, j0, nj, acc[z, :m_rows])

    def second(ref, u, i, mirror):
        g = jnp.concatenate([gc[i * per + k, part] for part in range(2) for k in range(per)], axis=0)
        here = pl.ds(pl.multiple_of(i * unit, unit), unit)
        at = pl.ds(pl.multiple_of(xor(c // per, u, n_units) * unit, unit), unit)
        block = dot_nt(ref[...].reshape(4 * unit, cols), g)
        sums, turns = [], []
        for z in range(2):
            by_re = block[2 * z * unit:(2 * z + 1) * unit]
            by_im = block[(2 * z + 1) * unit:(2 * z + 2) * unit]
            sums.append(by_re[:, :unit] + by_im[:, unit:])
            turns.append(by_re[:, unit:] - by_im[:, :unit])
        for part in range(2):
            turn = turns[0] if part else -turns[1]
            focal[part, at, here] += sums[part] + turn
            if mirror:
                focal[part, here, at] += (sums[part] - turn).T

    def diagonal(u):
        for t in range(n_tiles):
            at_r = columns(h * n_tiles + t)
            for k in range(per):
                j = u * per + k
                left = gr[pl.ds(2 * j, 2), :, :, at_r].reshape(2 * quarter, TILE)
                for z in range(2):
                    keep(y_diag, j, z, columns(t), dot_nn(left, d_buf[t, z]), 0)

    def unit_there(k):
        return xor(c // per, k, n_units)

    def pairs(p):
        for k in range(p + 1):
            second(y.at[p], p, unit_there(k), True)
        for u in range(p):
            second(y.at[u], u, unit_there(p), True)

    def diagonal_part(early):
        split = n_units - 1
        ahead = look(lambda chip: int(chip in plan.early)) == 1

        def fill(units, others):
            @pl.loop(*units)
            def _(u):
                diagonal(u)
                for k in range(*others):
                    second(y_diag, u, unit_there(k), False)

        if early:
            pl.when(ahead)(lambda: fill((0, split), (0, split)))
        else:
            @pl.when(ahead)
            def _():
                fill((0, split), (split, n_units))
                fill((split, n_units), (0, n_units))

            pl.when(jnp.logical_not(ahead))(lambda: fill((0, n_units), (0, n_units)))

    for part in range(2):
        @pl.when(user)
        def _():
            focal[part] = jnp.zeros_like(focal[part])

    def local_wait(j):
        for half in range(2):
            to_local(j, half).wait()

    groups = [[0], [1, 2]] + ([list(range(3, n))] if n > 3 else [])
    for stage, group in enumerate(groups):
        if stage == 2 and per == 1:
            pl.when(on_diag)(lambda: diagonal_part(True))
        for j in group:
            if stage:
                pl.when(user)(functools.partial(take, j))
            pl.when(on_diag)(functools.partial(twin, j))
            if j < group[-1] and per == 1:
                first_diag(j, 1)

                @pl.when(on_diag)
                def _():
                    local_wait(j)
                    pairs(j)
        if stage:
            for valid, copy in own_sends(stage - 1):
                pl.when(valid & drained(stage - 1))(copy.wait_send)
            begin(stage)
            pass_on(stage - 1)
        for j in group:
            pl.when(full)(functools.partial(twin, j))
        first(group[0], len(group))
        if per == 1:
            first_diag(group[-1], 1)

            @pl.when(on_diag)
            def _():
                local_wait(group[-1])
                pairs(group[-1])
        else:
            first_diag(group[0], len(group))
    pass_on(2)

    @pl.when(full)
    def _():
        @pl.loop(0, n // per)
        def _(i):
            slot = jnp.int32(0)
            waits = jnp.bool_(False)
            for k in range(n // per):
                slot = jnp.where(i == k, look(lambda key: plan.order[key][k]), slot)
                waits = waits | ((i == k) & (look(lambda key: plan.waits[key][k], 1) == 1))

            @pl.when(waits)
            def _():
                for k in range(per):
                    col_arrival(slot * per + k, 0).wait_recv()
                    col_arrival(slot * per + k, 1).wait_recv()

            for u in range(n_units):
                second(y.at[u], u, slot, True)

    @pl.when(on_diag)
    def _():
        if per == 1:
            diagonal_part(False)
        else:
            for j in range(n):
                local_wait(j)

            @pl.loop(0, n_units)
            def _(u):
                diagonal(u)

                @pl.loop(0, n_units)
                def _(k):
                    second(y.at[u], u, k, True)
                    second(y_diag, u, k, False)

    share = n_dev // 2
    group = max(16, out_rows)
    each = group // out_rows
    n_groups = n_p // group // 2

    def rows_of(half, g):
        return pl.ds(pl.multiple_of((half * n_groups + g) * group, group), group)

    def slab_pair(start):
        return pltpu.make_async_remote_copy(
            src_ref=slab.at[pl.ds(start, share)], dst_ref=pair, send_sem=pair_send, recv_sem=pair_recv,
            device_id=(r, 2 * c + 1 - h), device_id_type=MESH,
        )

    def slab_to(i):
        other = h * share + i
        return pltpu.make_async_remote_copy(
            src_ref=slab.at[other], dst_ref=arrived.at[chip], send_sem=slab_send.at[i],
            recv_sem=slab_recv.at[chip],
            device_id=(other // n_src, lax.rem(other, n_src)), device_id_type=MESH,
        )

    def slab_from(z, b):
        return pltpu.make_async_remote_copy(
            src_ref=slab.at[0], dst_ref=arrived.at[z * n + b], send_sem=slab_send.at[0],
            recv_sem=slab_recv.at[z * n + b], device_id=(z, 2 * b + me // share), device_id_type=MESH,
        )

    @pl.when(user)
    def _():
        @pl.loop(0, n_groups)
        def _(g):
            for part in range(2):
                block = focal[part, rows_of(1 - h, g), :]
                for j in range(each):
                    slab[(1 - h) * share + g * each + j, :, part * n_p:(part + 1) * n_p] = block[
                        j * out_rows:(j + 1) * out_rows
                    ].astype(bf16)

        slab_pair((1 - h) * share).start()
        slab_pair(0).wait_recv()

        def begin_slab(i):
            @pl.when(h * share + i != me)
            def _():
                slab_to(i).start()

        @pl.loop(0, n_groups)
        def _(g):
            for part in range(2):
                block = focal[part, rows_of(h, g), :]
                for j in range(each):
                    at = slice(part * n_p, (part + 1) * n_p)
                    slab[h * share + g * each + j, :, at] = (
                        block[j * out_rows:(j + 1) * out_rows] + pair[g * each + j, :, at].astype(f32)
                    ).astype(bf16)

            @pl.when(g > 0)
            def _():
                for j in range(each):
                    begin_slab((g - 1) * each + j)

        for j in range(each):
            begin_slab(share - each + j)

    focal_ref[...] = jnp.zeros_like(focal_ref)
    own_half = h == me // share

    @pl.when(user & own_half)
    def _():
        focal_ref[...] = slab[me].astype(f32)

    for z in range(n):
        for b in range(z, n):
            @pl.when(jnp.logical_not(own_half & (chip == z * n + b)))
            def _():
                slab_from(z, b).wait_recv()
                focal_ref[...] += arrived[z * n + b].astype(f32)

    real, imag = focal_ref[:, :n_p], focal_ref[:, n_p:]
    chosen = lax.broadcasted_iota(jnp.int32, (out_rows, n_p), 1) == index_ref[...]
    anchor_real = jnp.sum(jnp.where(chosen, real, 0.0), axis=1, keepdims=True)
    anchor_imag = jnp.sum(jnp.where(chosen, imag, 0.0), axis=1, keepdims=True)
    out_ref[:, 0, :] = real * anchor_real + imag * anchor_imag
    out_ref[:, 1, :] = imag * anchor_real - real * anchor_imag

    @pl.when(user)
    def _():
        slab_pair((1 - h) * share).wait_send()

        @pl.loop(0, share)
        def _(i):
            @pl.when(h * share + i != me)
            def _():
                slab_to(i).wait_send()

    for point in range(3):
        for valid, copy in own_sends(point):
            if point < 2:
                valid = valid & jnp.logical_not(drained(point))
            pl.when(valid)(copy.wait_send)
    for stage in range(3):
        for i in range(width(plan.step[stage])):
            for half in range(2):
                valid, _, _, copy = step_to(stage, i, half)
                pl.when(valid)(copy.wait_send)

    @pl.when(user)
    def _():
        for j in range(n):
            to_partner(j).wait_send()
            for i in range(relays(j)):
                valid, copy = relay_to(j, i)
                pl.when(valid)(copy.wait_send)
            for half in range(2):
                for i in range(downs(j)):
                    valid, copy = down_to(j, i, half)
                    pl.when(valid)(copy.wait_send)


def body(reflection, green, tile_mask, reference_index):
    rows, cols = reflection.shape[1], reflection.shape[2]
    n_rcv, n_src = lax.axis_size("rcv"), lax.axis_size("src")
    n_dev = n_rcv * n_src
    own_p = green.shape[2]
    n_p = own_p * n_src
    out_rows = n_p // n_dev
    n = n_src // 2
    assert n == n_rcv and rows == 2 * cols
    n_tiles = cols // TILE
    unit = max(2 * own_p, 128)
    piece = jnp.swapaxes(green, 1, 2)
    dma = pltpu.SemaphoreType.DMA
    any_spec = pl.BlockSpec(memory_space=pl.ANY)
    return pl.pallas_call(
        functools.partial(kernel, n_rcv, n_src),
        out_shape=jax.ShapeDtypeStruct((out_rows, 2, n_p), f32),
        in_specs=[
            pl.BlockSpec(memory_space=pltpu.SMEM), pl.BlockSpec(memory_space=pltpu.VMEM), any_spec, any_spec,
        ],
        out_specs=pl.BlockSpec(memory_space=pltpu.VMEM),
        scratch_shapes=[
            pltpu.VMEM((out_rows, 2 * n_p), f32),
            pltpu.VMEM((n_tiles, 2, rows, TILE), bf16),
            pltpu.VMEM((n_tiles, 2, TILE, TILE), bf16),
            pltpu.VMEM((n_src, 2, own_p, rows), bf16),
            pltpu.VMEM((n, 2, 2 * own_p, cols), bf16),
            pltpu.VMEM((n_p // unit, 2, 2, unit, cols), bf16),
            pltpu.VMEM((2, 2, unit, cols), bf16),
            pltpu.VMEM((2, 4 * own_p * max(2, n - 3), TILE), f32),
            pltpu.VMEM((2, n_p, n_p), f32),
            pltpu.VMEM((n_dev, out_rows, 2 * n_p), bf16),
            pltpu.VMEM((n_dev // 2, out_rows, 2 * n_p), bf16),
            pltpu.VMEM((n_dev // 2, out_rows, 2 * n_p), bf16),
            dma((n_tiles,)), dma, dma((3, n)), dma((n,)), dma((n, n)), dma((n_src,)),
            dma((3, 2 * n, 2)), dma((n, n, 2)), dma((3, 2 * n, 2)), dma((n_src,)), dma((n, 2)), dma((n_dev // 2,)), dma((n_dev // 2,)),
            dma, dma,
        ],
        compiler_params=pltpu.CompilerParams(
            collective_id=0, has_side_effects=True, vmem_limit_bytes=63 * 1024 * 1024
        ),
        name="focus",
    )(tile_mask, reference_index[:, None], piece, reflection)


def solution(mesh):
    return jax.shard_map(
        body,
        mesh=mesh,
        in_specs=(P(None, "rcv", "src"), P(None, "rcv", "src"), P(), P(("rcv", "src"))),
        out_specs=P(("rcv", "src"), None, None),
        check_vma=False,
    )
```

```python
import functools

import jax
import jax.numpy as jnp
from jax import lax
from jax.experimental import pallas as pl
from jax.experimental.pallas import tpu as pltpu
from jax.sharding import PartitionSpec as P

MESH = pl.DeviceIdType.MESH
TILE = 256
f32 = jnp.float32
bf16 = jnp.bfloat16


def dot_nn(a, b):
    return lax.dot_general(a, b, (((1,), (0,)), ((), ())), preferred_element_type=f32)


def dot_nt(a, b):
    return lax.dot_general(a, b, (((1,), (1,)), ((), ())), preferred_element_type=f32)


ROW = [
    {(0, 0): [1, 2], (0, 1): [0, 3], (0, 2): [3, 0], (0, 3): [2, 1], (1, 0): [1, 2], (1, 1): [3], (1, 2): [3], (1, 3): [2, 1], (2, 0): [2], (2, 1): [3], (2, 2): [3], (2, 3): [2], (3, 0): [3], (3, 1): [3], (3, 2): [3]},
    {},
    {},
]
COL = [
    {(1, 0): [(0, 1, 0)], (1, 1): [(0, 1, 1)], (2, 0): [(1, 0, 0)], (2, 1): [(1, 2, 1)], (2, 2): [(0, 2, 2)], (3, 0): [(1, 0, 1)], (3, 1): [(2, 1, 0)], (3, 3): [(0, 3, 3)]},
    {(3, 0): [(2, 3, 0)], (3, 1): [(1, 3, 1)], (3, 2): [(2, 3, 2)]},
    {},
]
RELAY = {((0, 1), 2): [0], ((0, 2), 2): [3], ((0, 3), 2): [2], ((0, 3), 1): [1], ((1, 2), 2): [3], ((1, 3), 2): [2], ((1, 3), 1): [1], ((2, 2), 2): [3], ((2, 3), 2): [2]}
DOWN = {((1, 1), 3): [0], ((1, 1), 2): [0], ((2, 2), 3): [0], ((2, 2), 1): [0], ((3, 3), 2): [0], ((3, 3), 1): [0]}
STEP = [
    {(0, 2): [(2, 1, 2, 2, 1)], (0, 3): [(3, 1, 3, 3, 1)], (1, 0): [(0, 0, 2, 0, 1), (0, 1, 2, 0, 0), (1, 0, 3, 0, 1), (1, 1, 3, 0, 0)], (1, 3): [(3, 2, 3, 3, 1)], (2, 1): [(0, 2, 3, 1, 1)]},
    {(0, 2): [(3, 1, 2, 3, 1)], (0, 3): [(2, 1, 3, 2, 1)]},
    {},
]
ORDER = {(0, 1): [1, 0, 3, 2], (0, 2): [2, 3, 0, 1], (0, 3): [3, 2, 1, 0], (1, 2): [1, 2, 0, 3], (1, 3): [3, 2, 1, 0], (2, 3): [2, 0, 3, 1]}
EARLY = [(0, 0), (2, 2), (3, 3)]


class Plan:
    def __init__(self, n):
        self.n = n
        self.row, self.col, self.step = ([{}, {}, {}] for _ in range(3))
        self.relay, self.down, self.order = {}, {}, {}
        self.early = []
        chips = [(z, c) for z in range(n) for c in range(n)]
        if n == 4:
            for point in range(3):
                self.row[point] = ROW[point]
                self.col[point] = COL[point]
                self.step[point] = STEP[point]
            self.relay, self.down, self.order, self.early = RELAY, DOWN, ORDER, EARLY
        else:
            for z, c in chips:
                self.row[0][z, c] = [t for t in sorted(range(z, n), key=lambda t: t ^ c) if t != c]
                self.col[0][z, c] = [(t, z, c) for t in range(z)]
        waited = {chip: {op[0] for stage in self.step for op in stage.get(chip, []) if op[4]} for chip in chips}
        order = {chip: self.order.get(chip, list(range(n))) for chip in chips}
        self.order = order
        self.waits = {chip: [int(q not in waited[chip]) for q in order[chip]] for chip in chips}

    def table(self, get):
        n = self.n
        return [get((i // n, i % n)) for i in range(n * n)]


def xor(a, b, n):
    out, bit = 0, 1
    while bit < n:
        out = out + bit * lax.rem(a // bit + b // bit, 2)
        bit *= 2
    return out


def kernel(
    n_rcv, n_src, mask_ref, index_ref, piece_ref, refl_ref, out_ref,
    focal_ref, a_buf, d_buf, gr, gc, y, y_diag, acc, focal, slab, pair, arrived,
    load_sem, own_sem, row_send, pass_send, relay_send, gr_recv,
    col_send, down_send, step_send, gc_recv, gc_local, slab_send, slab_recv,
    pair_send, pair_recv,
):
    n_dev = n_rcv * n_src
    n = n_src // 2
    plan = Plan(n)
    r = lax.axis_index("rcv")
    s = lax.axis_index("src")
    me = r * n_src + s
    c = s // 2
    h = lax.rem(s, 2)
    chip = r * n + c
    own_p, rows = gr.shape[2], gr.shape[3]
    n_p = own_p * n_src
    cols = gc.shape[3]
    out_rows = n_p // n_dev
    quarter = 2 * own_p
    n_tiles, row_tiles = cols // TILE, rows // TILE
    user = c >= r
    on_diag = c == r
    full = c > r

    def look(get, default=0):
        value = jnp.int32(default)
        for i, entry in enumerate(plan.table(get)):
            if entry != default:
                value = jnp.where(chip == i, entry, value)
        return value

    def width(lists):
        return max([len(ops) for ops in lists.values()] + [0])

    def entry(lists, i, field=None, default=-1):
        def get(key):
            ops = lists.get(key, [])
            if i >= len(ops):
                return default
            return ops[i] if field is None else ops[i][field]

        return get

    def load(t):
        return pltpu.make_async_copy(
            refl_ref.at[:, :, pl.ds(t * TILE, TILE)], a_buf.at[t], load_sem.at[t]
        )

    own_copy = pltpu.make_async_copy(piece_ref, gr.at[h], own_sem)

    @pl.when(user)
    def _():
        own_copy.start()
        for t in range(n_tiles):
            load(t).start()

    barrier = pltpu.get_barrier_semaphore()

    @pl.loop(1, n_dev)
    def _(i):
        other = lax.rem(me + i, n_dev)
        pl.semaphore_signal(
            barrier, inc=1, device_id=(other // n_src, lax.rem(other, n_src)), device_id_type=MESH
        )

    pl.semaphore_wait(barrier, n_dev - 1)

    def row_to(point, i):
        to = look(entry(plan.row[point], i))
        slot = 2 * xor(c, to, n) + h
        return to >= 0, pltpu.make_async_remote_copy(
            src_ref=piece_ref, dst_ref=gr.at[slot], send_sem=row_send.at[point, i], recv_sem=gr_recv.at[slot],
            device_id=(r, 2 * to + h), device_id_type=MESH,
        )

    def to_partner(j):
        slot = 2 * j + h
        src = piece_ref if j == 0 else gr.at[slot]
        return pltpu.make_async_remote_copy(
            src_ref=src, dst_ref=gr.at[slot], send_sem=pass_send.at[j], recv_sem=gr_recv.at[slot],
            device_id=(r, 2 * c + 1 - h), device_id_type=MESH,
        )

    def arrival(slot):
        return pltpu.make_async_remote_copy(
            src_ref=piece_ref, dst_ref=gr.at[slot], send_sem=pass_send.at[0], recv_sem=gr_recv.at[slot],
            device_id=(r, 2 * c + 1 - h), device_id_type=MESH,
        )

    def relay_to(j, i):
        lists = {key[0]: ops for key, ops in plan.relay.items() if key[1] == j}
        to = look(entry(lists, i))
        slot = 2 * j + h
        there = 2 * xor(xor(c, j, n), to, n) + h
        return to >= 0, pltpu.make_async_remote_copy(
            src_ref=gr.at[slot], dst_ref=gr.at[there], send_sem=relay_send.at[j, i],
            recv_sem=gr_recv.at[there], device_id=(r, 2 * to + h), device_id_type=MESH,
        )

    def relays(j):
        return width({key: ops for key, ops in plan.relay.items() if key[1] == j})

    def col_part(ref_slot, half):
        return gc.at[ref_slot, :, pl.ds(pl.multiple_of(half * own_p, own_p), own_p), :]

    def col_to(point, i, k):
        lists = plan.col[point]
        z = look(entry(lists, i, 0))
        to = look(entry(lists, i, 1))
        slot = look(entry(lists, i, 2))
        return z >= 0, pltpu.make_async_remote_copy(
            src_ref=piece_ref.at[:, :, pl.ds(k * cols, cols)], dst_ref=col_part(slot, h),
            send_sem=col_send.at[point, i, k], recv_sem=gc_recv.at[2 * slot + h],
            device_id=(z, 2 * to + k), device_id_type=MESH,
        )

    def down_to(j, i, half):
        lists = {key[0]: ops for key, ops in plan.down.items() if key[1] == j}
        z = look(entry(lists, i))
        q = xor(c, j, n)
        return z >= 0, pltpu.make_async_remote_copy(
            src_ref=gr.at[2 * j + half, :, :, pl.ds(pl.multiple_of(h * cols, cols), cols)],
            dst_ref=col_part(q, half), send_sem=down_send.at[j, i, half], recv_sem=gc_recv.at[2 * q + half],
            device_id=(z, s), device_id_type=MESH,
        )

    def downs(j):
        return width({key: ops for key, ops in plan.down.items() if key[1] == j})

    def step_to(stage, i, half):
        lists = plan.step[stage]
        slot = look(entry(lists, i, 0))
        there = look(entry(lists, i, 3))
        return slot >= 0, look(entry(lists, i, 4)) == 1, slot, pltpu.make_async_remote_copy(
            src_ref=col_part(slot, half), dst_ref=col_part(there, half),
            send_sem=step_send.at[stage, i, half], recv_sem=gc_recv.at[2 * there + half],
            device_id=(look(entry(lists, i, 1)), 2 * look(entry(lists, i, 2)) + h), device_id_type=MESH,
        )

    def col_arrival(slot, half):
        return pltpu.make_async_remote_copy(
            src_ref=piece_ref.at[:, :, pl.ds(0, cols)], dst_ref=col_part(slot, half),
            send_sem=col_send.at[0, 0, 0], recv_sem=gc_recv.at[2 * slot + half],
            device_id=(r, 2 * c + 1 - h), device_id_type=MESH,
        )

    def to_local(j, half):
        q = xor(c, j, n)
        return pltpu.make_async_copy(
            gr.at[2 * j + half, :, :, pl.ds(pl.multiple_of(h * cols, cols), cols)],
            col_part(q, half), gc_local.at[j, half],
        )

    def pass_on(stage):
        for i in range(width(plan.step[stage])):
            for half in range(2):
                valid, waits, slot, copy = step_to(stage, i, half)

                @pl.when(valid)
                def _():
                    @pl.when(waits)
                    def _():
                        col_arrival(slot, half).wait_recv()

                    copy.start()

    @pl.when(user)
    def _():
        to_partner(0).start()

    def own_sends(point):
        ops = [row_to(point, i) for i in range(width(plan.row[point]))]
        return ops + [col_to(point, i, k) for i in range(width(plan.col[point])) for k in range(2)]

    def begin(point):
        for valid, copy in own_sends(point):
            pl.when(valid)(copy.start)

    def drained(point):
        later = plan.row[point + 1], plan.col[point + 1]
        return look(lambda chip: int(chip[1] < chip[0] and any(lists.get(chip) for lists in later))) == 1

    begin(0)

    @pl.when(user)
    def _():
        own_copy.wait()

    def take(j):
        arrival(2 * j + h).wait_recv()
        to_partner(j).start()
        for i in range(relays(j)):
            valid, copy = relay_to(j, i)
            pl.when(valid)(copy.start)

    def twin(j):
        arrival(2 * j + 1 - h).wait_recv()
        for half in range(2):
            for i in range(downs(j)):
                valid, copy = down_to(j, i, half)
                pl.when(valid)(copy.start)

            @pl.when(on_diag)
            def _():
                to_local(j, half).start()

    step_rows = min(rows, 1024)
    step_tiles = step_rows // TILE

    def clean(t):
        @pl.when(on_diag)
        def _():
            at = pl.ds(pl.multiple_of((h * n_tiles + t) * TILE, TILE), TILE)
            m = mask_ref[(r * row_tiles + h * n_tiles) + t, s * n_tiles + t]
            for z in range(2):
                tile = a_buf[t, z, at, :]
                d_buf[t, z] = jnp.where(m == 1, tile, jnp.zeros_like(tile))
                a_buf[t, z, at, :] = jnp.zeros_like(tile)

        for j in range(row_tiles):
            m = mask_ref[r * row_tiles + j, s * n_tiles + t]
            at = pl.ds(j * TILE, TILE)
            for z in range(2):
                tile = a_buf[t, z, at, :]
                a_buf[t, z, at, :] = jnp.where(m == 1, tile, jnp.zeros_like(tile))

    unit = max(quarter, 128)
    per = unit // quarter
    n_units = n // per

    def keep(ref, j, z, at, block, start):
        block = block.astype(bf16)
        inner = xor(c, j, n) % per if per > 1 else 0
        for half in range(2):
            for part in range(2):
                begin = start + (half * 2 + part) * own_p
                rows_at = pl.ds(pl.multiple_of(inner * quarter + half * own_p, own_p), own_p)
                ref[z, part, rows_at, at] = block[begin:begin + own_p]

    def columns(t):
        return pl.ds(pl.multiple_of(t * TILE, TILE), TILE)

    def keep_all(z, t, j0, nj, block):
        for j in range(nj):
            keep(y.at[(j0 + j) // per], j0 + j, z, columns(t), block, j * 2 * quarter)

    def first(j0, nj):
        m_rows = nj * 2 * quarter

        @pl.when(full)
        def _():
            @pl.loop(0, n_tiles)
            def _(t):
                if j0 == 0:
                    load(t).wait()
                    clean(t)
                left = gr[2 * j0:2 * (j0 + nj)].reshape(m_rows, rows)
                for z in range(2):
                    keep_all(z, t, j0, nj, dot_nn(left, a_buf[t, z]))

    def first_diag(j0, nj):
        m_rows = nj * 2 * quarter

        @pl.when(on_diag)
        def _():
            @pl.loop(0, n_tiles)
            def _(t):
                if j0 == 0:
                    load(t).wait()
                    clean(t)
                col_end = h * cols + (t + 1) * TILE
                for k in range(rows // step_rows):
                    def step():
                        left = gr[2 * j0:2 * (j0 + nj), :, :, k * step_rows:(k + 1) * step_rows]
                        left = left.reshape(m_rows, step_rows)
                        for z in range(2):
                            term = dot_nn(left, a_buf[t, z, k * step_rows:(k + 1) * step_rows, :])
                            if k == 0:
                                acc[z, :m_rows] = term
                            else:
                                acc[z, :m_rows] += term

                    if k == 0:
                        step()
                    else:
                        pl.when(k * step_rows < col_end)(step)
                for z in range(2):
                    keep_all(z, t, j0, nj, acc[z, :m_rows])

    def second(ref, u, i, mirror):
        g = jnp.concatenate([gc[i * per + k, part] for part in range(2) for k in range(per)], axis=0)
        here = pl.ds(pl.multiple_of(i * unit, unit), unit)
        at = pl.ds(pl.multiple_of(xor(c // per, u, n_units) * unit, unit), unit)
        block = dot_nt(ref[...].reshape(4 * unit, cols), g)
        sums, turns = [], []
        for z in range(2):
            by_re = block[2 * z * unit:(2 * z + 1) * unit]
            by_im = block[(2 * z + 1) * unit:(2 * z + 2) * unit]
            sums.append(by_re[:, :unit] + by_im[:, unit:])
            turns.append(by_re[:, unit:] - by_im[:, :unit])
        for part in range(2):
            turn = turns[0] if part else -turns[1]
            focal[part, at, here] += sums[part] + turn
            if mirror:
                focal[part, here, at] += (sums[part] - turn).T

    def diagonal(u):
        for t in range(n_tiles):
            at_r = columns(h * n_tiles + t)
            for k in range(per):
                j = u * per + k
                left = gr[pl.ds(2 * j, 2), :, :, at_r].reshape(2 * quarter, TILE)
                for z in range(2):
                    keep(y_diag, j, z, columns(t), dot_nn(left, d_buf[t, z]), 0)

    def unit_there(k):
        return xor(c // per, k, n_units)

    def pairs(p):
        for k in range(p + 1):
            second(y.at[p], p, unit_there(k), True)
        for u in range(p):
            second(y.at[u], u, unit_there(p), True)

    def diagonal_part(early):
        split = n_units - 1
        ahead = look(lambda chip: int(chip in plan.early)) == 1

        def fill(units, others):
            @pl.loop(*units)
            def _(u):
                diagonal(u)
                for k in range(*others):
                    second(y_diag, u, unit_there(k), False)

        if early:
            pl.when(ahead)(lambda: fill((0, split), (0, split)))
        else:
            @pl.when(ahead)
            def _():
                fill((0, split), (split, n_units))
                fill((split, n_units), (0, n_units))

            pl.when(jnp.logical_not(ahead))(lambda: fill((0, n_units), (0, n_units)))

    for part in range(2):
        @pl.when(user)
        def _():
            focal[part] = jnp.zeros_like(focal[part])

    def local_wait(j):
        for half in range(2):
            to_local(j, half).wait()

    groups = [[0], [1, 2]] + ([list(range(3, n))] if n > 3 else [])
    for stage, group in enumerate(groups):
        if stage == 2 and per == 1:
            pl.when(on_diag)(lambda: diagonal_part(True))
        for j in group:
            if stage:
                pl.when(user)(functools.partial(take, j))
            pl.when(on_diag)(functools.partial(twin, j))
            if j < group[-1] and per == 1:
                first_diag(j, 1)

                @pl.when(on_diag)
                def _():
                    local_wait(j)
                    pairs(j)
        if stage:
            for valid, copy in own_sends(stage - 1):
                pl.when(valid & drained(stage - 1))(copy.wait_send)
            begin(stage)
            pass_on(stage - 1)
        for j in group:
            pl.when(full)(functools.partial(twin, j))
        first(group[0], len(group))
        if per == 1:
            first_diag(group[-1], 1)

            @pl.when(on_diag)
            def _():
                local_wait(group[-1])
                pairs(group[-1])
        else:
            first_diag(group[0], len(group))
    pass_on(2)

    @pl.when(full)
    def _():
        @pl.loop(0, n // per)
        def _(i):
            slot = jnp.int32(0)
            waits = jnp.bool_(False)
            for k in range(n // per):
                slot = jnp.where(i == k, look(lambda key: plan.order[key][k]), slot)
                waits = waits | ((i == k) & (look(lambda key: plan.waits[key][k], 1) == 1))

            @pl.when(waits)
            def _():
                for k in range(per):
                    col_arrival(slot * per + k, 0).wait_recv()
                    col_arrival(slot * per + k, 1).wait_recv()

            for u in range(n_units):
                second(y.at[u], u, slot, True)

    @pl.when(on_diag)
    def _():
        if per == 1:
            diagonal_part(False)
        else:
            for j in range(n):
                local_wait(j)

            @pl.loop(0, n_units)
            def _(u):
                diagonal(u)

                @pl.loop(0, n_units)
                def _(k):
                    second(y.at[u], u, k, True)
                    second(y_diag, u, k, False)

    share = n_dev // 2
    group = max(16, out_rows)
    each = group // out_rows
    n_groups = n_p // group // 2

    def rows_of(half, g):
        return pl.ds(pl.multiple_of((half * n_groups + g) * group, group), group)

    def slab_pair(start):
        return pltpu.make_async_remote_copy(
            src_ref=slab.at[pl.ds(start, share)], dst_ref=pair, send_sem=pair_send, recv_sem=pair_recv,
            device_id=(r, 2 * c + 1 - h), device_id_type=MESH,
        )

    def slab_to(i):
        other = h * share + i
        return pltpu.make_async_remote_copy(
            src_ref=slab.at[other], dst_ref=arrived.at[chip], send_sem=slab_send.at[i],
            recv_sem=slab_recv.at[chip],
            device_id=(other // n_src, lax.rem(other, n_src)), device_id_type=MESH,
        )

    def slab_from(z, b):
        return pltpu.make_async_remote_copy(
            src_ref=slab.at[0], dst_ref=arrived.at[z * n + b], send_sem=slab_send.at[0],
            recv_sem=slab_recv.at[z * n + b], device_id=(z, 2 * b + me // share), device_id_type=MESH,
        )

    @pl.when(user)
    def _():
        @pl.loop(0, n_groups)
        def _(g):
            for part in range(2):
                block = focal[part, rows_of(1 - h, g), :]
                for j in range(each):
                    slab[(1 - h) * share + g * each + j, :, part * n_p:(part + 1) * n_p] = block[
                        j * out_rows:(j + 1) * out_rows
                    ].astype(bf16)

        slab_pair((1 - h) * share).start()
        slab_pair(0).wait_recv()

        def begin_slab(i):
            @pl.when(h * share + i != me)
            def _():
                slab_to(i).start()

        @pl.loop(0, n_groups)
        def _(g):
            for part in range(2):
                block = focal[part, rows_of(h, g), :]
                for j in range(each):
                    at = slice(part * n_p, (part + 1) * n_p)
                    slab[h * share + g * each + j, :, at] = (
                        block[j * out_rows:(j + 1) * out_rows] + pair[g * each + j, :, at].astype(f32)
                    ).astype(bf16)

            @pl.when(g > 0)
            def _():
                for j in range(each):
                    begin_slab((g - 1) * each + j)

        for j in range(each):
            begin_slab(share - each + j)

    focal_ref[...] = jnp.zeros_like(focal_ref)
    own_half = h == me // share

    @pl.when(user & own_half)
    def _():
        focal_ref[...] = slab[me].astype(f32)

    for z in range(n):
        for b in range(z, n):
            @pl.when(jnp.logical_not(own_half & (chip == z * n + b)))
            def _():
                slab_from(z, b).wait_recv()
                focal_ref[...] += arrived[z * n + b].astype(f32)

    real, imag = focal_ref[:, :n_p], focal_ref[:, n_p:]
    chosen = lax.broadcasted_iota(jnp.int32, (out_rows, n_p), 1) == index_ref[...]
    anchor_real = jnp.sum(jnp.where(chosen, real, 0.0), axis=1, keepdims=True)
    anchor_imag = jnp.sum(jnp.where(chosen, imag, 0.0), axis=1, keepdims=True)
    out_ref[:, 0, :] = real * anchor_real + imag * anchor_imag
    out_ref[:, 1, :] = imag * anchor_real - real * anchor_imag

    @pl.when(user)
    def _():
        slab_pair((1 - h) * share).wait_send()

        @pl.loop(0, share)
        def _(i):
            @pl.when(h * share + i != me)
            def _():
                slab_to(i).wait_send()

    for point in range(3):
        for valid, copy in own_sends(point):
            if point < 2:
                valid = valid & jnp.logical_not(drained(point))
            pl.when(valid)(copy.wait_send)
    for stage in range(3):
        for i in range(width(plan.step[stage])):
            for half in range(2):
                valid, _, _, copy = step_to(stage, i, half)
                pl.when(valid)(copy.wait_send)

    @pl.when(user)
    def _():
        for j in range(n):
            to_partner(j).wait_send()
            for i in range(relays(j)):
                valid, copy = relay_to(j, i)
                pl.when(valid)(copy.wait_send)
            for half in range(2):
                for i in range(downs(j)):
                    valid, copy = down_to(j, i, half)
                    pl.when(valid)(copy.wait_send)


def body(reflection, green, tile_mask, reference_index):
    rows, cols = reflection.shape[1], reflection.shape[2]
    n_rcv, n_src = lax.axis_size("rcv"), lax.axis_size("src")
    n_dev = n_rcv * n_src
    own_p = green.shape[2]
    n_p = own_p * n_src
    out_rows = n_p // n_dev
    n = n_src // 2
    assert n == n_rcv and rows == 2 * cols
    n_tiles = cols // TILE
    unit = max(2 * own_p, 128)
    piece = jnp.swapaxes(green, 1, 2)
    dma = pltpu.SemaphoreType.DMA
    any_spec = pl.BlockSpec(memory_space=pl.ANY)
    return pl.pallas_call(
        functools.partial(kernel, n_rcv, n_src),
        out_shape=jax.ShapeDtypeStruct((out_rows, 2, n_p), f32),
        in_specs=[
            pl.BlockSpec(memory_space=pltpu.SMEM), pl.BlockSpec(memory_space=pltpu.VMEM), any_spec, any_spec,
        ],
        out_specs=pl.BlockSpec(memory_space=pltpu.VMEM),
        scratch_shapes=[
            pltpu.VMEM((out_rows, 2 * n_p), f32),
            pltpu.VMEM((n_tiles, 2, rows, TILE), bf16),
            pltpu.VMEM((n_tiles, 2, TILE, TILE), bf16),
            pltpu.VMEM((n_src, 2, own_p, rows), bf16),
            pltpu.VMEM((n, 2, 2 * own_p, cols), bf16),
            pltpu.VMEM((n_p // unit, 2, 2, unit, cols), bf16),
            pltpu.VMEM((2, 2, unit, cols), bf16),
            pltpu.VMEM((2, 4 * own_p * max(2, n - 3), TILE), f32),
            pltpu.VMEM((2, n_p, n_p), f32),
            pltpu.VMEM((n_dev, out_rows, 2 * n_p), bf16),
            pltpu.VMEM((n_dev // 2, out_rows, 2 * n_p), bf16),
            pltpu.VMEM((n_dev // 2, out_rows, 2 * n_p), bf16),
            dma((n_tiles,)), dma, dma((3, n)), dma((n,)), dma((n, n)), dma((n_src,)),
            dma((3, 2 * n, 2)), dma((n, n, 2)), dma((3, 2 * n, 2)), dma((n_src,)), dma((n, 2)), dma((n_dev // 2,)), dma((n_dev // 2,)),
            dma, dma,
        ],
        compiler_params=pltpu.CompilerParams(
            collective_id=0, has_side_effects=True, vmem_limit_bytes=63 * 1024 * 1024
        ),
        name="focus",
    )(tile_mask, reference_index[:, None], piece, reflection)


def solution(mesh):
    return jax.shard_map(
        body,
        mesh=mesh,
        in_specs=(P(None, "rcv", "src"), P(None, "rcv", "src"), P(), P(("rcv", "src"))),
        out_specs=P(("rcv", "src"), None, None),
        check_vma=False,
    )
```

```python
import functools

import jax
import jax.numpy as jnp
from jax import lax
from jax.experimental import pallas as pl
from jax.experimental.pallas import tpu as pltpu
from jax.sharding import PartitionSpec as P

MESH = pl.DeviceIdType.MESH
TILE = 256
f32 = jnp.float32
bf16 = jnp.bfloat16


def dot_nn(a, b):
    return lax.dot_general(a, b, (((1,), (0,)), ((), ())), preferred_element_type=f32)


def dot_nt(a, b):
    return lax.dot_general(a, b, (((1,), (1,)), ((), ())), preferred_element_type=f32)


ROW = [
    {(0, 0): [1, 2], (0, 1): [0, 3], (0, 2): [3, 0], (0, 3): [2, 1], (1, 0): [1, 2], (1, 1): [3], (1, 2): [3], (1, 3): [2, 1], (2, 0): [2], (2, 1): [3], (2, 2): [3], (2, 3): [2], (3, 1): [3], (3, 2): [3]},
    {(3, 0): [3]},
    {},
]
COL = [
    {(1, 0): [(0, 1, 0)], (1, 1): [(0, 1, 1)], (2, 0): [(1, 0, 2)], (2, 1): [(1, 0, 1)], (2, 2): [(0, 2, 2)], (3, 0): [(1, 0, 0)], (3, 1): [(2, 0, 0), (2, 1, 0)], (3, 3): [(0, 3, 3)]},
    {(3, 2): [(2, 3, 2)]},
    {},
]
RELAY = {((0, 1), 2): [0], ((0, 2), 2): [3], ((0, 3), 2): [2], ((0, 3), 1): [1], ((1, 2), 2): [3], ((1, 3), 2): [2], ((1, 3), 1): [1], ((2, 2), 2): [3], ((2, 3), 2): [2]}
DOWN = {((1, 1), 2): [0], ((1, 1), 3): [0], ((2, 2), 1): [0], ((2, 2), 3): [0], ((3, 3), 2): [0], ((3, 3), 1): [0]}
STEP = [
    {(0, 2): [(2, 1, 2, 2, 1)], (0, 3): [(3, 1, 3, 3, 1)], (1, 0): [(0, 1, 3, 0, 1), (1, 1, 2, 1, 1), (2, 0, 2, 0, 1), (0, 0, 3, 0, 0), (2, 1, 2, 0, 0), (0, 2, 3, 0, 0)], (2, 0): [(0, 1, 3, 1, 1)], (2, 1): [(0, 2, 3, 1, 1)]},
    {(0, 2): [(3, 1, 2, 3, 1)], (0, 3): [(2, 1, 3, 2, 1)], (1, 3): [(3, 2, 3, 3, 1)]},
    {},
]
ORDER = {(0, 1): [1, 0, 3, 2], (0, 2): [2, 3, 0, 1], (0, 3): [3, 2, 1, 0], (1, 2): [2, 1, 0, 3], (1, 3): [0, 3, 1, 2], (2, 3): [2, 0, 3, 1]}
EARLY = [(0, 0), (2, 2), (3, 3)]


class Plan:
    def __init__(self, n):
        self.n = n
        self.row, self.col, self.step = ([{}, {}, {}] for _ in range(3))
        self.relay, self.down, self.order = {}, {}, {}
        self.early = []
        chips = [(z, c) for z in range(n) for c in range(n)]
        if n == 4:
            for point in range(3):
                self.row[point] = ROW[point]
                self.col[point] = COL[point]
                self.step[point] = STEP[point]
            self.relay, self.down, self.order, self.early = RELAY, DOWN, ORDER, EARLY
        else:
            for z, c in chips:
                self.row[0][z, c] = [t for t in sorted(range(z, n), key=lambda t: t ^ c) if t != c]
                self.col[0][z, c] = [(t, z, c) for t in range(z)]
        waited = {chip: {op[0] for stage in self.step for op in stage.get(chip, []) if op[4]} for chip in chips}
        order = {chip: self.order.get(chip, list(range(n))) for chip in chips}
        self.order = order
        self.waits = {chip: [int(q not in waited[chip]) for q in order[chip]] for chip in chips}

    def table(self, get):
        n = self.n
        return [get((i // n, i % n)) for i in range(n * n)]


def xor(a, b, n):
    out, bit = 0, 1
    while bit < n:
        out = out + bit * lax.rem(a // bit + b // bit, 2)
        bit *= 2
    return out


def kernel(
    n_rcv, n_src, mask_ref, index_ref, piece_ref, refl_ref, out_ref,
    focal_ref, a_buf, d_buf, gr, gc, y, y_diag, acc, focal, slab, pair, arrived,
    load_sem, own_sem, row_send, pass_send, relay_send, gr_recv,
    col_send, down_send, step_send, gc_recv, gc_local, slab_send, slab_recv,
    pair_send, pair_recv,
):
    n_dev = n_rcv * n_src
    n = n_src // 2
    plan = Plan(n)
    r = lax.axis_index("rcv")
    s = lax.axis_index("src")
    me = r * n_src + s
    c = s // 2
    h = lax.rem(s, 2)
    chip = r * n + c
    own_p, rows = gr.shape[2], gr.shape[3]
    n_p = own_p * n_src
    cols = gc.shape[3]
    out_rows = n_p // n_dev
    quarter = 2 * own_p
    n_tiles, row_tiles = cols // TILE, rows // TILE
    user = c >= r
    on_diag = c == r
    full = c > r

    def look(get, default=0):
        value = jnp.int32(default)
        for i, entry in enumerate(plan.table(get)):
            if entry != default:
                value = jnp.where(chip == i, entry, value)
        return value

    def width(lists):
        return max([len(ops) for ops in lists.values()] + [0])

    def entry(lists, i, field=None, default=-1):
        def get(key):
            ops = lists.get(key, [])
            if i >= len(ops):
                return default
            return ops[i] if field is None else ops[i][field]

        return get

    def load(t):
        return pltpu.make_async_copy(
            refl_ref.at[:, :, pl.ds(t * TILE, TILE)], a_buf.at[t], load_sem.at[t]
        )

    own_copy = pltpu.make_async_copy(piece_ref, gr.at[h], own_sem)

    @pl.when(user)
    def _():
        own_copy.start()
        for t in range(n_tiles):
            load(t).start()

    barrier = pltpu.get_barrier_semaphore()

    @pl.loop(1, n_dev)
    def _(i):
        other = lax.rem(me + i, n_dev)
        pl.semaphore_signal(
            barrier, inc=1, device_id=(other // n_src, lax.rem(other, n_src)), device_id_type=MESH
        )

    pl.semaphore_wait(barrier, n_dev - 1)

    def row_to(point, i):
        to = look(entry(plan.row[point], i))
        slot = 2 * xor(c, to, n) + h
        return to >= 0, pltpu.make_async_remote_copy(
            src_ref=piece_ref, dst_ref=gr.at[slot], send_sem=row_send.at[point, i], recv_sem=gr_recv.at[slot],
            device_id=(r, 2 * to + h), device_id_type=MESH,
        )

    def to_partner(j):
        slot = 2 * j + h
        src = piece_ref if j == 0 else gr.at[slot]
        return pltpu.make_async_remote_copy(
            src_ref=src, dst_ref=gr.at[slot], send_sem=pass_send.at[j], recv_sem=gr_recv.at[slot],
            device_id=(r, 2 * c + 1 - h), device_id_type=MESH,
        )

    def arrival(slot):
        return pltpu.make_async_remote_copy(
            src_ref=piece_ref, dst_ref=gr.at[slot], send_sem=pass_send.at[0], recv_sem=gr_recv.at[slot],
            device_id=(r, 2 * c + 1 - h), device_id_type=MESH,
        )

    def relay_to(j, i):
        lists = {key[0]: ops for key, ops in plan.relay.items() if key[1] == j}
        to = look(entry(lists, i))
        slot = 2 * j + h
        there = 2 * xor(xor(c, j, n), to, n) + h
        return to >= 0, pltpu.make_async_remote_copy(
            src_ref=gr.at[slot], dst_ref=gr.at[there], send_sem=relay_send.at[j, i],
            recv_sem=gr_recv.at[there], device_id=(r, 2 * to + h), device_id_type=MESH,
        )

    def relays(j):
        return width({key: ops for key, ops in plan.relay.items() if key[1] == j})

    def col_part(ref_slot, half):
        return gc.at[ref_slot, :, pl.ds(pl.multiple_of(half * own_p, own_p), own_p), :]

    def col_to(point, i, k):
        lists = plan.col[point]
        z = look(entry(lists, i, 0))
        to = look(entry(lists, i, 1))
        slot = look(entry(lists, i, 2))
        return z >= 0, pltpu.make_async_remote_copy(
            src_ref=piece_ref.at[:, :, pl.ds(k * cols, cols)], dst_ref=col_part(slot, h),
            send_sem=col_send.at[point, i, k], recv_sem=gc_recv.at[2 * slot + h],
            device_id=(z, 2 * to + k), device_id_type=MESH,
        )

    def down_to(j, i, half):
        lists = {key[0]: ops for key, ops in plan.down.items() if key[1] == j}
        z = look(entry(lists, i))
        q = xor(c, j, n)
        return z >= 0, pltpu.make_async_remote_copy(
            src_ref=gr.at[2 * j + half, :, :, pl.ds(pl.multiple_of(h * cols, cols), cols)],
            dst_ref=col_part(q, half), send_sem=down_send.at[j, i, half], recv_sem=gc_recv.at[2 * q + half],
            device_id=(z, s), device_id_type=MESH,
        )

    def downs(j):
        return width({key: ops for key, ops in plan.down.items() if key[1] == j})

    def step_to(stage, i, half):
        lists = plan.step[stage]
        slot = look(entry(lists, i, 0))
        there = look(entry(lists, i, 3))
        return slot >= 0, look(entry(lists, i, 4)) == 1, slot, pltpu.make_async_remote_copy(
            src_ref=col_part(slot, half), dst_ref=col_part(there, half),
            send_sem=step_send.at[stage, i, half], recv_sem=gc_recv.at[2 * there + half],
            device_id=(look(entry(lists, i, 1)), 2 * look(entry(lists, i, 2)) + h), device_id_type=MESH,
        )

    def col_arrival(slot, half):
        return pltpu.make_async_remote_copy(
            src_ref=piece_ref.at[:, :, pl.ds(0, cols)], dst_ref=col_part(slot, half),
            send_sem=col_send.at[0, 0, 0], recv_sem=gc_recv.at[2 * slot + half],
            device_id=(r, 2 * c + 1 - h), device_id_type=MESH,
        )

    def to_local(j, half):
        q = xor(c, j, n)
        return pltpu.make_async_copy(
            gr.at[2 * j + half, :, :, pl.ds(pl.multiple_of(h * cols, cols), cols)],
            col_part(q, half), gc_local.at[j, half],
        )

    def pass_on(stage):
        for i in range(width(plan.step[stage])):
            for half in range(2):
                valid, waits, slot, copy = step_to(stage, i, half)

                @pl.when(valid)
                def _():
                    @pl.when(waits)
                    def _():
                        col_arrival(slot, half).wait_recv()

                    copy.start()

    @pl.when(user)
    def _():
        to_partner(0).start()

    def own_sends(point):
        ops = [row_to(point, i) for i in range(width(plan.row[point]))]
        return ops + [col_to(point, i, k) for i in range(width(plan.col[point])) for k in range(2)]

    def begin(point):
        for valid, copy in own_sends(point):
            pl.when(valid)(copy.start)

    def drained(point):
        later = plan.row[point + 1], plan.col[point + 1]
        return look(lambda chip: int(chip[1] < chip[0] and any(lists.get(chip) for lists in later))) == 1

    begin(0)

    @pl.when(user)
    def _():
        own_copy.wait()

    def take(j):
        arrival(2 * j + h).wait_recv()
        to_partner(j).start()
        for i in range(relays(j)):
            valid, copy = relay_to(j, i)
            pl.when(valid)(copy.start)

    def twin(j):
        arrival(2 * j + 1 - h).wait_recv()
        for half in range(2):
            for i in range(downs(j)):
                valid, copy = down_to(j, i, half)
                pl.when(valid)(copy.start)

            @pl.when(on_diag)
            def _():
                to_local(j, half).start()

    step_rows = min(rows, 1024)
    step_tiles = step_rows // TILE

    def clean(t):
        @pl.when(on_diag)
        def _():
            at = pl.ds(pl.multiple_of((h * n_tiles + t) * TILE, TILE), TILE)
            m = mask_ref[(r * row_tiles + h * n_tiles) + t, s * n_tiles + t]
            for z in range(2):
                tile = a_buf[t, z, at, :]
                d_buf[t, z] = jnp.where(m == 1, tile, jnp.zeros_like(tile))
                a_buf[t, z, at, :] = jnp.zeros_like(tile)

        for j in range(row_tiles):
            m = mask_ref[r * row_tiles + j, s * n_tiles + t]
            at = pl.ds(j * TILE, TILE)
            for z in range(2):
                tile = a_buf[t, z, at, :]
                a_buf[t, z, at, :] = jnp.where(m == 1, tile, jnp.zeros_like(tile))

    unit = max(quarter, 128)
    per = unit // quarter
    n_units = n // per

    def keep(ref, j, z, at, block, start):
        block = block.astype(bf16)
        inner = xor(c, j, n) % per if per > 1 else 0
        for half in range(2):
            for part in range(2):
                begin = start + (half * 2 + part) * own_p
                rows_at = pl.ds(pl.multiple_of(inner * quarter + half * own_p, own_p), own_p)
                ref[z, part, rows_at, at] = block[begin:begin + own_p]

    def columns(t):
        return pl.ds(pl.multiple_of(t * TILE, TILE), TILE)

    def keep_all(z, t, j0, nj, block):
        for j in range(nj):
            keep(y.at[(j0 + j) // per], j0 + j, z, columns(t), block, j * 2 * quarter)

    def first(j0, nj):
        m_rows = nj * 2 * quarter

        @pl.when(full)
        def _():
            @pl.loop(0, n_tiles)
            def _(t):
                if j0 == 0:
                    load(t).wait()
                    clean(t)
                left = gr[2 * j0:2 * (j0 + nj)].reshape(m_rows, rows)
                for z in range(2):
                    keep_all(z, t, j0, nj, dot_nn(left, a_buf[t, z]))

    def first_diag(j0, nj):
        m_rows = nj * 2 * quarter

        @pl.when(on_diag)
        def _():
            @pl.loop(0, n_tiles)
            def _(t):
                if j0 == 0:
                    load(t).wait()
                    clean(t)
                col_end = h * cols + (t + 1) * TILE
                for k in range(rows // step_rows):
                    def step():
                        left = gr[2 * j0:2 * (j0 + nj), :, :, k * step_rows:(k + 1) * step_rows]
                        left = left.reshape(m_rows, step_rows)
                        for z in range(2):
                            term = dot_nn(left, a_buf[t, z, k * step_rows:(k + 1) * step_rows, :])
                            if k == 0:
                                acc[z, :m_rows] = term
                            else:
                                acc[z, :m_rows] += term

                    if k == 0:
                        step()
                    else:
                        pl.when(k * step_rows < col_end)(step)
                for z in range(2):
                    keep_all(z, t, j0, nj, acc[z, :m_rows])

    def second(ref, u, i, mirror):
        g = jnp.concatenate([gc[i * per + k, part] for part in range(2) for k in range(per)], axis=0)
        here = pl.ds(pl.multiple_of(i * unit, unit), unit)
        at = pl.ds(pl.multiple_of(xor(c // per, u, n_units) * unit, unit), unit)
        block = dot_nt(ref[...].reshape(4 * unit, cols), g)
        sums, turns = [], []
        for z in range(2):
            by_re = block[2 * z * unit:(2 * z + 1) * unit]
            by_im = block[(2 * z + 1) * unit:(2 * z + 2) * unit]
            sums.append(by_re[:, :unit] + by_im[:, unit:])
            turns.append(by_re[:, unit:] - by_im[:, :unit])
        for part in range(2):
            turn = turns[0] if part else -turns[1]
            focal[part, at, here] += sums[part] + turn
            if mirror:
                focal[part, here, at] += (sums[part] - turn).T

    def diagonal(u):
        for t in range(n_tiles):
            at_r = columns(h * n_tiles + t)
            for k in range(per):
                j = u * per + k
                left = gr[pl.ds(2 * j, 2), :, :, at_r].reshape(2 * quarter, TILE)
                for z in range(2):
                    keep(y_diag, j, z, columns(t), dot_nn(left, d_buf[t, z]), 0)

    def unit_there(k):
        return xor(c // per, k, n_units)

    def pairs(p):
        for k in range(p + 1):
            second(y.at[p], p, unit_there(k), True)
        for u in range(p):
            second(y.at[u], u, unit_there(p), True)

    def diagonal_part(early):
        split = n_units - 1
        ahead = look(lambda chip: int(chip in plan.early)) == 1

        def fill(units, others):
            @pl.loop(*units)
            def _(u):
                diagonal(u)
                for k in range(*others):
                    second(y_diag, u, unit_there(k), False)

        if early:
            pl.when(ahead)(lambda: fill((0, split), (0, split)))
        else:
            @pl.when(ahead)
            def _():
                fill((0, split), (split, n_units))
                fill((split, n_units), (0, n_units))

            pl.when(jnp.logical_not(ahead))(lambda: fill((0, n_units), (0, n_units)))

    for part in range(2):
        @pl.when(user)
        def _():
            focal[part] = jnp.zeros_like(focal[part])

    def local_wait(j):
        for half in range(2):
            to_local(j, half).wait()

    groups = [[0], [1, 2]] + ([list(range(3, n))] if n > 3 else [])
    for stage, group in enumerate(groups):
        if stage == 2 and per == 1:
            pl.when(on_diag)(lambda: diagonal_part(True))
        for j in group:
            if stage:
                pl.when(user)(functools.partial(take, j))
            pl.when(on_diag)(functools.partial(twin, j))
            if j < group[-1] and per == 1:
                first_diag(j, 1)

                @pl.when(on_diag)
                def _():
                    local_wait(j)
                    pairs(j)
        if stage:
            for valid, copy in own_sends(stage - 1):
                pl.when(valid & drained(stage - 1))(copy.wait_send)
            begin(stage)
            pass_on(stage - 1)
        for j in group:
            pl.when(full)(functools.partial(twin, j))
        first(group[0], len(group))
        if per == 1:
            first_diag(group[-1], 1)

            @pl.when(on_diag)
            def _():
                local_wait(group[-1])
                pairs(group[-1])
        else:
            first_diag(group[0], len(group))
    pass_on(2)

    @pl.when(full)
    def _():
        @pl.loop(0, n // per)
        def _(i):
            slot = jnp.int32(0)
            waits = jnp.bool_(False)
            for k in range(n // per):
                slot = jnp.where(i == k, look(lambda key: plan.order[key][k]), slot)
                waits = waits | ((i == k) & (look(lambda key: plan.waits[key][k], 1) == 1))

            @pl.when(waits)
            def _():
                for k in range(per):
                    col_arrival(slot * per + k, 0).wait_recv()
                    col_arrival(slot * per + k, 1).wait_recv()

            for u in range(n_units):
                second(y.at[u], u, slot, True)

    @pl.when(on_diag)
    def _():
        if per == 1:
            diagonal_part(False)
        else:
            for j in range(n):
                local_wait(j)

            @pl.loop(0, n_units)
            def _(u):
                diagonal(u)

                @pl.loop(0, n_units)
                def _(k):
                    second(y.at[u], u, k, True)
                    second(y_diag, u, k, False)

    share = n_dev // 2
    group = max(16, out_rows)
    each = group // out_rows
    n_groups = n_p // group // 2

    def rows_of(half, g):
        return pl.ds(pl.multiple_of((half * n_groups + g) * group, group), group)

    def slab_pair(start):
        return pltpu.make_async_remote_copy(
            src_ref=slab.at[pl.ds(start, share)], dst_ref=pair, send_sem=pair_send, recv_sem=pair_recv,
            device_id=(r, 2 * c + 1 - h), device_id_type=MESH,
        )

    def slab_to(i):
        other = h * share + i
        return pltpu.make_async_remote_copy(
            src_ref=slab.at[other], dst_ref=arrived.at[chip], send_sem=slab_send.at[i],
            recv_sem=slab_recv.at[chip],
            device_id=(other // n_src, lax.rem(other, n_src)), device_id_type=MESH,
        )

    def slab_from(z, b):
        return pltpu.make_async_remote_copy(
            src_ref=slab.at[0], dst_ref=arrived.at[z * n + b], send_sem=slab_send.at[0],
            recv_sem=slab_recv.at[z * n + b], device_id=(z, 2 * b + me // share), device_id_type=MESH,
        )

    @pl.when(user)
    def _():
        @pl.loop(0, n_groups)
        def _(g):
            for part in range(2):
                block = focal[part, rows_of(1 - h, g), :]
                for j in range(each):
                    slab[(1 - h) * share + g * each + j, :, part * n_p:(part + 1) * n_p] = block[
                        j * out_rows:(j + 1) * out_rows
                    ].astype(bf16)

        slab_pair((1 - h) * share).start()
        slab_pair(0).wait_recv()

        def begin_slab(i):
            @pl.when(h * share + i != me)
            def _():
                slab_to(i).start()

        @pl.loop(0, n_groups)
        def _(g):
            for part in range(2):
                block = focal[part, rows_of(h, g), :]
                for j in range(each):
                    at = slice(part * n_p, (part + 1) * n_p)
                    slab[h * share + g * each + j, :, at] = (
                        block[j * out_rows:(j + 1) * out_rows] + pair[g * each + j, :, at].astype(f32)
                    ).astype(bf16)

            @pl.when(g > 0)
            def _():
                for j in range(each):
                    begin_slab((g - 1) * each + j)

        for j in range(each):
            begin_slab(share - each + j)

    focal_ref[...] = jnp.zeros_like(focal_ref)
    own_half = h == me // share

    @pl.when(user & own_half)
    def _():
        focal_ref[...] = slab[me].astype(f32)

    for z in range(n):
        for b in range(z, n):
            @pl.when(jnp.logical_not(own_half & (chip == z * n + b)))
            def _():
                slab_from(z, b).wait_recv()
                focal_ref[...] += arrived[z * n + b].astype(f32)

    real, imag = focal_ref[:, :n_p], focal_ref[:, n_p:]
    chosen = lax.broadcasted_iota(jnp.int32, (out_rows, n_p), 1) == index_ref[...]
    anchor_real = jnp.sum(jnp.where(chosen, real, 0.0), axis=1, keepdims=True)
    anchor_imag = jnp.sum(jnp.where(chosen, imag, 0.0), axis=1, keepdims=True)
    out_ref[:, 0, :] = real * anchor_real + imag * anchor_imag
    out_ref[:, 1, :] = imag * anchor_real - real * anchor_imag

    @pl.when(user)
    def _():
        slab_pair((1 - h) * share).wait_send()

        @pl.loop(0, share)
        def _(i):
            @pl.when(h * share + i != me)
            def _():
                slab_to(i).wait_send()

    for point in range(3):
        for valid, copy in own_sends(point):
            if point < 2:
                valid = valid & jnp.logical_not(drained(point))
            pl.when(valid)(copy.wait_send)
    for stage in range(3):
        for i in range(width(plan.step[stage])):
            for half in range(2):
                valid, _, _, copy = step_to(stage, i, half)
                pl.when(valid)(copy.wait_send)

    @pl.when(user)
    def _():
        for j in range(n):
            to_partner(j).wait_send()
            for i in range(relays(j)):
                valid, copy = relay_to(j, i)
                pl.when(valid)(copy.wait_send)
            for half in range(2):
                for i in range(downs(j)):
                    valid, copy = down_to(j, i, half)
                    pl.when(valid)(copy.wait_send)


def body(reflection, green, tile_mask, reference_index):
    rows, cols = reflection.shape[1], reflection.shape[2]
    n_rcv, n_src = lax.axis_size("rcv"), lax.axis_size("src")
    n_dev = n_rcv * n_src
    own_p = green.shape[2]
    n_p = own_p * n_src
    out_rows = n_p // n_dev
    n = n_src // 2
    assert n == n_rcv and rows == 2 * cols
    n_tiles = cols // TILE
    unit = max(2 * own_p, 128)
    piece = jnp.swapaxes(green, 1, 2)
    dma = pltpu.SemaphoreType.DMA
    any_spec = pl.BlockSpec(memory_space=pl.ANY)
    return pl.pallas_call(
        functools.partial(kernel, n_rcv, n_src),
        out_shape=jax.ShapeDtypeStruct((out_rows, 2, n_p), f32),
        in_specs=[
            pl.BlockSpec(memory_space=pltpu.SMEM), pl.BlockSpec(memory_space=pltpu.VMEM), any_spec, any_spec,
        ],
        out_specs=pl.BlockSpec(memory_space=pltpu.VMEM),
        scratch_shapes=[
            pltpu.VMEM((out_rows, 2 * n_p), f32),
            pltpu.VMEM((n_tiles, 2, rows, TILE), bf16),
            pltpu.VMEM((n_tiles, 2, TILE, TILE), bf16),
            pltpu.VMEM((n_src, 2, own_p, rows), bf16),
            pltpu.VMEM((n, 2, 2 * own_p, cols), bf16),
            pltpu.VMEM((n_p // unit, 2, 2, unit, cols), bf16),
            pltpu.VMEM((2, 2, unit, cols), bf16),
            pltpu.VMEM((2, 4 * own_p * max(2, n - 3), TILE), f32),
            pltpu.VMEM((2, n_p, n_p), f32),
            pltpu.VMEM((n_dev, out_rows, 2 * n_p), bf16),
            pltpu.VMEM((n_dev // 2, out_rows, 2 * n_p), bf16),
            pltpu.VMEM((n_dev // 2, out_rows, 2 * n_p), bf16),
            dma((n_tiles,)), dma, dma((3, n)), dma((n,)), dma((n, n)), dma((n_src,)),
            dma((3, 2 * n, 2)), dma((n, n, 2)), dma((3, 2 * n, 2)), dma((n_src,)), dma((n, 2)), dma((n_dev // 2,)), dma((n_dev // 2,)),
            dma, dma,
        ],
        compiler_params=pltpu.CompilerParams(
            collective_id=0, has_side_effects=True, vmem_limit_bytes=63 * 1024 * 1024
        ),
        name="focus",
    )(tile_mask, reference_index[:, None], piece, reflection)


def solution(mesh):
    return jax.shard_map(
        body,
        mesh=mesh,
        in_specs=(P(None, "rcv", "src"), P(None, "rcv", "src"), P(), P(("rcv", "src"))),
        out_specs=P(("rcv", "src"), None, None),
        check_vma=False,
    )
```
